128 devices in a mesh: corpus: 32 (over y, z, core), query: 4 (over x).
Axes of the slice: x: 4, y: 4, z: 4, core: 2. Of those that a mesh axis runs over, the one named last changes fastest.
Arguments:
- queries: bfloat16 [32768, 768], P(('corpus', 'query')), may hold values from -8 to 8
- probes: int32 [32768, 4], P(('corpus', 'query')), may hold values from 0 to 1023, as said below
- targets: int32 [32768, 8], P(('corpus', 'query')), may hold values from 0 to 4095, all different within a row
- passage_codes: int32 [1024, 96, 1024], P('corpus'), may hold values from 0 to 15
- codebook: float32 [16, 768], replicated, may hold values from -6 to 6
Outputs:
- grad_queries: bfloat16 [32768, 768], P(('corpus', 'query'))
- codebook_step: float32 [16, 768], replicated
The draws below stay inside these ranges and needn't reach their ends.
Inputs may be any that keep to these rules, and one draw needn't show every extreme that they name: `probes`: each row names 4 different lists; list l belongs to index l // 32 of corpus. In every aligned block of 256 rows (the rows of one device) no list is named more than 2 times, and one list, the same one in every block, is named exactly 2 times. `targets`: each row names 8 different candidates; column r holds the candidate of rank r.
All inputs are finite; a program needn't handle non-finite values.
Results may differ from the reference program's by a relative error of at most 0.01.
The reference program's roundings to bfloat16 on the way count: a program that leaves them out, or rounds other values in their place, can miss the bound.
Values may be sent and summed in bfloat16 or wider, within the bound.
No kernel may reach another device: no remote copies, remote signals or barrier semaphores. Data moves between devices by JAX's collectives and lax.ppermute only.
A program may use at most 192 MiB of HBM per device.

```python
import math
import jax
import jax.numpy as jnp
import numpy as np
from jax import lax

D = 768
SUBSPACES = 96
CENTROIDS = 16
SUBDIM = 8
PASSAGES = 1024
PROBES = 4
TARGETS = 8
Q_DEV = 256
LISTS = 1024
CAP = 2
QUERIES = 32768


def draw_queries(key, part):
    column_key = jax.random.fold_in(key, 11)
    spread = jnp.exp(jax.random.uniform(column_key, (D,), jnp.float32, jnp.log(0.01), jnp.log(0.1)))
    values = jax.random.truncated_normal(jax.random.fold_in(key, 17), -6.0, 6.0, (QUERIES, D), jnp.float32) * spread[None, :]
    return jnp.clip(values, -8.0, 8.0).astype(jnp.bfloat16)


def draw_probes(key, part):
    blocks = QUERIES // Q_DEV
    others = LISTS - 1
    hot_list = jax.random.randint(jax.random.fold_in(key, 21), (), 0, LISTS)

    def block_probes(block_key):
        sub_keys = jax.random.split(block_key, 4)
        list_cycle = jax.random.permutation(sub_keys[0], others).astype(jnp.int32)
        list_cycle = list_cycle + (list_cycle >= hot_list).astype(jnp.int32)
        offset = jax.random.randint(sub_keys[1], (), 0, others)
        row_order = jax.random.permutation(sub_keys[2], Q_DEV).astype(jnp.int32)
        row_rank = jnp.zeros((Q_DEV,), jnp.int32).at[row_order].set(jnp.arange(Q_DEV, dtype=jnp.int32))
        is_hot = row_rank < CAP
        first_entry = jnp.where(is_hot, (PROBES - 1) * row_rank, (PROBES - 1) * CAP + PROBES * (row_rank - CAP))
        probe_cols = jnp.arange(PROBES, dtype=jnp.int32)
        entry_index = first_entry[:, None] + jnp.where(is_hot[:, None], probe_cols[None, :] - 1, probe_cols[None, :])
        chosen = list_cycle[(entry_index + offset) % others]
        base_lists = jnp.where(is_hot[:, None] & (probe_cols == 0)[None, :], hot_list, chosen)
        rotation = jax.random.randint(sub_keys[3], (Q_DEV, 1), 0, PROBES)
        column_index = (probe_cols[None, :] - rotation) % PROBES
        return jnp.take_along_axis(base_lists, column_index, axis=1)
    block_keys = jax.random.split(jax.random.fold_in(key, 22), blocks)
    return jax.vmap(block_probes)(block_keys).reshape(QUERIES, PROBES).astype(jnp.int32)


def place_ends(drawn, rng, least, high):
    extent = drawn.shape
    index_at = [jax.random.randint(jax.random.fold_in(rng, axis), (), 0, extent[axis]) for axis in range(len(extent))]
    drawn = drawn.at[tuple(index_at)].set(least)
    longest = extent.index(max(extent))
    index_at[longest] = (index_at[longest] + 1) % extent[longest]
    return drawn.at[tuple(index_at)].set(high)


def cumulative_ranks(amount, lean):
    weights = [(1 << 20) // math.isqrt(grade ** lean) + 1 for grade in range(1, amount + 1)]
    scale = 1 + sum(weights) // (1 << 30)
    return np.cumsum(np.array([max(1, weight // scale) for weight in weights]))


def skewed_ids(own_key, shape, number_of, lean):
    listing = cumulative_ranks(number_of, lean)
    ticket = jax.random.randint(jax.random.fold_in(own_key, 1), shape, 0, int(listing[number_of - 1]))
    rank = jnp.searchsorted(jnp.asarray(listing, jnp.int32), ticket, side="right")
    return jax.random.permutation(jax.random.fold_in(own_key, 2), number_of)[rank].astype(jnp.int32)


def choose_distinct(stream_key, rows, count, top, lift):
    sequence = jax.random.permutation(jax.random.fold_in(stream_key, 1), count)
    favour = sequence
    for power in range(3):
        favour = favour * favour // count
    favour = favour * lift // count
    lots = jax.random.randint(jax.random.fold_in(stream_key, 2), (rows, count), 0, 4096) + favour
    fixed_rows = jax.random.permutation(jax.random.fold_in(stream_key, 3), rows)[jnp.arange(count) % rows]
    lots = jnp.where(jnp.arange(rows)[:, None] == fixed_rows[None, :], 1 << 14, lots)
    score = lots * count + jnp.arange(count)
    return lax.top_k(score.astype(jnp.int32), top)[1].astype(jnp.int32)


def bell_draw(key, dims, scale, bound, held_as=jnp.bfloat16):
    return jnp.clip(scale * jax.random.normal(key, dims, jnp.float32), -bound, bound).astype(held_as)


def setup_inputs(seed: int = 0) -> dict:
    keys = jax.random.split(jax.random.key(seed), 6)
    queries = draw_queries(jax.random.fold_in(keys[5], 71), 0)
    probes = draw_probes(jax.random.fold_in(keys[5], 71), 0)
    targets = choose_distinct(keys[2], QUERIES, PROBES * PASSAGES, TARGETS, 0)
    passage_codes = place_ends(skewed_ids(keys[3], (LISTS, SUBSPACES, PASSAGES), CENTROIDS, 2), jax.random.fold_in(keys[3], 3), 0, CENTROIDS - 1).astype(jnp.int32)
    codebook = bell_draw(keys[4], (CENTROIDS, D), 1.0, 6.0, jnp.float32)
    return dict(queries=queries, probes=probes, targets=targets, passage_codes=passage_codes, codebook=codebook)


EPSILON = 1e-06
NEGATIVE = -1e+30

def rank_weights():
    levels = jnp.arange(TARGETS).astype(jnp.int32).astype(jnp.float32)
    return 2.0 * (TARGETS - levels) / (TARGETS * (TARGETS + 1.0))

def centroid_table(code_list):
    levels = jnp.arange(CENTROIDS).astype(jnp.int32)
    marked = code_list[:, None, :] == levels[None, :, None]
    return marked.astype(jnp.float32).reshape(SUBSPACES * CENTROIDS, PASSAGES)

def reference(queries, probes, targets, passage_codes, codebook):
    highest = lax.Precision.HIGHEST
    blocks = QUERIES // Q_DEV
    per_block = Q_DEV * PROBES
    entries = QUERIES * PROBES
    column_cap = blocks * CAP
    centroids = codebook.reshape(CENTROIDS, SUBSPACES, SUBDIM)
    split_queries = queries.astype(jnp.float32).reshape(QUERIES, SUBSPACES, SUBDIM)
    lookup = jnp.einsum('qme,kme->qmk', split_queries, centroids, precision=highest)
    lookup = lookup.reshape(QUERIES, SUBSPACES * CENTROIDS).astype(jnp.bfloat16)
    list_ids = jnp.arange(LISTS).astype(jnp.int32)

    def block_ranks(block_probes):
        marked = (block_probes[:, None] == list_ids[None, :]).astype(jnp.int32)
        running = jnp.cumsum(marked, axis=0)
        return lax.optimization_barrier(jnp.sum(marked * running, axis=1)) - 1
    flat_probes = probes.reshape(blocks, per_block)
    block_rank = lax.map(block_ranks, flat_probes)
    block_index = jnp.arange(blocks).astype(jnp.int32)[:, None]
    position = (flat_probes * column_cap + block_index * CAP + block_rank).reshape(entries)
    entry_at = jnp.full((LISTS * column_cap,), -1, jnp.int32).at[position].set(jnp.arange(entries).astype(jnp.int32))
    probe_cols = jnp.arange(PROBES).astype(jnp.int32)
    inside = targets[:, None, :] // PASSAGES == probe_cols[None, :, None]
    target_spot = jnp.where(inside, targets[:, None, :] % PASSAGES, -1).reshape(entries, TARGETS)
    weights = rank_weights()
    places = jnp.arange(PASSAGES).astype(jnp.int32)

    def list_scores(list_index):
        owned_ids = lax.dynamic_slice_in_dim(entry_at, list_index * column_cap, column_cap)
        is_valid = owned_ids >= 0
        safe_id = jnp.maximum(owned_ids, 0)
        lut_rows = lookup[safe_id // PROBES].astype(jnp.float32)
        one_hot = centroid_table(passage_codes[list_index])
        scores = jnp.dot(lut_rows, one_hot, precision=highest)
        return (is_valid, safe_id, scores, one_hot)

    def first_pass(list_index):
        is_valid, safe_id, scores, one_hot = list_scores(list_index)
        top_score = lax.optimization_barrier(jnp.max(scores, axis=1))
        exp_total = lax.optimization_barrier(jnp.sum(jnp.exp(scores - top_score[:, None]), axis=1))
        return (jnp.where(is_valid, top_score, NEGATIVE), jnp.where(is_valid, exp_total, 0.0))
    slot_top, slot_total = lax.map(first_pass, jnp.arange(LISTS).astype(jnp.int32))
    entry_top = slot_top.reshape(-1)[position].reshape(QUERIES, PROBES)
    entry_total = slot_total.reshape(-1)[position].reshape(QUERIES, PROBES)
    query_top = lax.optimization_barrier(jnp.max(entry_top, axis=1))
    query_total = lax.optimization_barrier(jnp.sum(entry_total * jnp.exp(entry_top - query_top[:, None]), axis=1))

    def second_pass(state_pair, list_index):
        grad_sum, book_sum = state_pair
        is_valid, safe_id, scores, one_hot = list_scores(list_index)
        owner_query = safe_id // PROBES
        spots = target_spot[safe_id]
        teacher = lax.optimization_barrier(jnp.sum(jnp.where(spots[:, :, None] == places[None, None, :], weights[None, :, None], 0.0), axis=1))
        student = jnp.exp(scores - query_top[owner_query][:, None]) / query_total[owner_query][:, None]
        grad_scores = jnp.where(is_valid[:, None], student - teacher, 0.0).astype(jnp.bfloat16)
        histogram = jnp.dot(grad_scores.astype(jnp.float32), one_hot.T, precision=highest)
        histogram = histogram.reshape(column_cap, SUBSPACES, CENTROIDS)
        partial_value = jnp.einsum('rmk,kme->rme', histogram, centroids, precision=highest).reshape(column_cap, D)
        grad_sum = grad_sum.at[owner_query].add(jnp.where(is_valid[:, None], partial_value, 0.0))
        chosen_rows = split_queries[owner_query]
        book_sum = book_sum + jnp.einsum('rmk,rme->kme', histogram, chosen_rows, precision=highest)
        return ((grad_sum, book_sum), None)
    initial = (jnp.zeros((QUERIES, D), jnp.float32), jnp.zeros((CENTROIDS, SUBSPACES, SUBDIM), jnp.float32))
    (grad_sum, book_sum), ignored = lax.scan(second_pass, initial, jnp.arange(LISTS).astype(jnp.int32))
    raw_grad = book_sum.reshape(CENTROIDS, D)
    normed = raw_grad * lax.rsqrt(jnp.mean(raw_grad * raw_grad) + EPSILON)
    return (grad_sum.astype(jnp.bfloat16), normed)
```

```python
import functools

import jax
import jax.numpy as jnp
from jax import lax
from jax.experimental import pallas as pl
from jax.experimental.pallas import tpu as pltpu
from jax.sharding import PartitionSpec as P

D = 768
SUBSPACES = 96
CENTROIDS = 16
SUBDIM = 8
PASSAGES = 1024
PROBES = 4
TARGETS = 8
CAP = 2
EPSILON = 1e-06

BOTH = ("corpus", "query")
CHUNKS = 6
FEATS = 128
ENTRIES = 256
WIDTH = SUBSPACES * CENTROIDS
F32 = jnp.float32
BF16 = jnp.bfloat16


def dot(a, b, dims=((1,), (0,))):
    return lax.dot_general(a, b, (dims, ((), ())), preferred_element_type=F32)


def iota(shape, axis):
    return lax.broadcasted_iota(jnp.int32, shape, axis)


def ones_where(mask):
    return jnp.where(mask, 1.0, 0.0).astype(BF16)


def split_two(value):
    high = value.astype(BF16)
    return high, (value - high.astype(F32)).astype(BF16)


def names_list(probe_rows, lists):
    found = probe_rows[0:1, :] == lists
    for p in range(1, PROBES):
        found = found | (probe_rows[p : p + 1, :] == lists)
    return found


def dispatch_body(probes_t, queries, sending):
    rows, count = sending.shape[0], queries.shape[0]
    slot = iota((rows, count), 0) + pl.program_id(0) * rows
    found = names_list(probes_t[...], slot >> 1)
    before = ones_where(iota((count, count), 0) < iota((count, count), 1))
    rank = dot(ones_where(found), before)
    chosen = ones_where(found & (rank == (slot & 1).astype(F32)))
    sending[...] = dot(chosen, queries[...]).astype(BF16)


def home_body(probes_t, probes, targets_wide, chosen_out, masks_out, notes_out):
    count = probes.shape[0]
    slots = chosen_out.shape[1]
    devices = notes_out.shape[0]
    per_device = masks_out.shape[0]
    block = 512
    after = ones_where(iota((count, count), 0) > iota((count, count), 1))
    for b in range(slots // block):
        slot = iota((count, block), 1) + b * block
        found = probes[:, 0:1] == (slot >> 1)
        for p in range(1, PROBES):
            found = found | (probes[:, p : p + 1] == (slot >> 1))
        rank = dot(after, ones_where(found))
        chosen_out[:, b * block : (b + 1) * block] = ones_where(
            found & (rank == (slot & 1).astype(F32))
        )
    wide = targets_wide[...]
    spot = wide & (PASSAGES - 1)
    column = wide // PASSAGES
    in_list = jnp.broadcast_to(probes[:, 0:1], wide.shape)
    for p in range(1, PROBES):
        in_list = jnp.where(column == p, probes[:, p : p + 1], in_list)
    parts = jnp.concatenate(
        [in_list >> 5, in_list & 31, spot >> 5, spot & 31], axis=1
    ).astype(F32).astype(BF16)
    before = ones_where(iota((count, count), 0) < iota((count, count), 1))
    lane = iota((devices, 128), 1)
    gathered = jnp.zeros((devices, 4 * 128), F32)
    lane_wide = iota((devices, 4 * 128), 1) & 127
    for i in range(per_device // 2):
        lists = iota((devices, count), 0) * (per_device // 2) + i
        found = names_list(probes_t[...], lists)
        rank = dot(ones_where(found), before)
        for r in range(2):
            mask = ones_where(found & (rank == float(r)))
            masks_out[2 * i + r] = mask
            here = dot(mask, parts)
            gathered = jnp.where(lane_wide // TARGETS == 2 * i + r, here, gathered)
    got_list = gathered[:, 0:128] * 32.0 + gathered[:, 128:256]
    got_spot = gathered[:, 256:384] * 32.0 + gathered[:, 384:512]
    own_list = iota((devices, 128), 0) * (per_device // 2) + lane // (2 * TARGETS)
    notes_out[...] = jnp.where(got_list == own_list.astype(F32), got_spot + 1.0, 0.0)


def fill_one_hot(codes, one_hot):
    for c in range(CHUNKS):
        part = codes[c * 16 : (c + 1) * 16, :].astype(F32).astype(BF16)
        for k in range(CENTROIDS):
            at = c * ENTRIES + k * 16
            one_hot[at : at + 16, :] = jnp.where(
                part == jnp.asarray(k, BF16), jnp.asarray(1, BF16), jnp.asarray(0, BF16)
            )


def score_body(offset, got, high, low, codes, exps, stats, table, one_hot):
    i = pl.program_id(0)
    half = got.shape[0] // (2 * 8)

    @pl.when(i == 0)
    def _():
        stats[...] = jnp.zeros_like(stats)
        for c in range(CHUNKS):
            rows = got[:, c * FEATS : (c + 1) * FEATS]
            twice = jnp.concatenate([rows, rows], axis=1)
            weights = jnp.concatenate([high[c], low[c]], axis=1)
            looked = dot(twice, weights, ((1,), (1,)))
            table[2 * c] = looked[:, 0:128]
            table[2 * c + 1] = looked[:, 128:256]

    fill_one_hot(codes.at[0], one_hot)
    rows = jnp.concatenate(
        [
            jnp.concatenate(
                [
                    table[j, pl.ds(2 * i + r, half, stride=16), :].astype(BF16)
                    for j in range(WIDTH // 128)
                ],
                axis=1,
            )
            for r in range(2)
        ],
        axis=0,
    )
    scores = dot(rows, one_hot[...])
    top = jnp.max(scores, axis=1, keepdims=True)
    exp_scores = jnp.exp(scores - top)
    total = jnp.sum(exp_scores, axis=1, keepdims=True)
    exps[0] = exp_scores
    lane = iota(stats.shape, 1)
    held = stats[...]
    for r in range(2):
        held = jnp.where(lane == 2 * i + r, top[r * half : (r + 1) * half], held)
        held = jnp.where(lane == 16 + 2 * i + r, total[r * half : (r + 1) * half], held)
    stats[...] = held


def weight_body(stats, masks, notes, message):
    per_device, devices, count = masks.shape
    low = -3.0e38
    peak = jnp.full((devices, count), low, F32)
    for s in range(per_device):
        peak = jnp.where(masks[s] > 0, stats[:, s : s + 1], peak) if s == 0 else jnp.maximum(
            peak, jnp.where(masks[s] > 0, stats[:, s : s + 1], low)
        )
    peak = jnp.max(peak, axis=0, keepdims=True)
    denom = jnp.zeros((devices, count), F32)
    for s in range(per_device):
        part = jnp.exp(stats[:, s : s + 1] - peak) * stats[:, 16 + s : 17 + s]
        denom = denom + jnp.where(masks[s] > 0, part, 0.0)
    denom = jnp.sum(denom, axis=0, keepdims=True)
    lane = iota((devices, 128), 1)
    held = jnp.zeros((devices, 128), F32)
    for s in range(per_device):
        part = jnp.exp(stats[:, s : s + 1] - peak) / denom
        part = jnp.sum(jnp.where(masks[s] > 0, part, 0.0), axis=1, keepdims=True)
        held = jnp.where(lane == s, part, held)
    message[:, 0:128] = held
    message[:, 128:256] = notes[...]


def grad_body(offset, exps, message, codes, got, high, low, part_out, book_out, hist, one_hot):
    i = pl.program_id(0)
    half = got.shape[0] // (2 * 8)
    fill_one_hot(codes.at[0], one_hot)
    turned = pltpu.roll(message[:, 128:256], (128 - 2 * TARGETS * i) % 128, 1)
    lane = iota((half, 128), 1)
    place = iota((half, PASSAGES), 1).astype(F32)
    grads = []
    for r in range(2):
        scale = jnp.sum(
            jnp.where(lane == 2 * i + r, message[:, 0:128], 0.0), axis=1, keepdims=True
        )
        teacher = jnp.zeros((half, PASSAGES), F32)
        for t in range(TARGETS):
            at = r * TARGETS + t
            weight = 2.0 * (TARGETS - t) / (TARGETS * (TARGETS + 1.0))
            teacher = jnp.where(place == turned[:, at : at + 1] - 1.0, weight, teacher)
        student = exps[0, r * half : (r + 1) * half, :] * scale
        grads.append((student - teacher).astype(BF16))
    grads = jnp.concatenate(grads, axis=0)
    found = dot(grads, one_hot[...], ((1,), (1,)))
    for r in range(2):
        for j in range(WIDTH // 128):
            hist[j, pl.ds(2 * i + r, half, stride=16), :] = found[
                r * half : (r + 1) * half, j * 128 : (j + 1) * 128
            ]

    @pl.when(i == pl.num_programs(0) - 1)
    def _():
        keep = iota((ENTRIES, FEATS), 0) % 16 == iota((ENTRIES, FEATS), 1) // SUBDIM
        for c in range(CHUNKS):
            h_high, h_low = split_two(jnp.concatenate([hist[2 * c], hist[2 * c + 1]], axis=1))
            both = jnp.concatenate([high[c], low[c]], axis=1)
            wide = dot(h_high, both)
            part = wide[:, 0:FEATS] + wide[:, FEATS:] + dot(h_low, high[c])
            part_out[:, c * FEATS : (c + 1) * FEATS] = part.astype(BF16)
            rows = got[:, c * FEATS : (c + 1) * FEATS]
            book = dot(rows, h_high, ((0,), (0,))) + dot(rows, h_low, ((0,), (0,)))
            book = jnp.where(keep, book.T, 0.0)
            book_out[:, c * FEATS : (c + 1) * FEATS] = jnp.sum(
                book.reshape(CENTROIDS, 16, FEATS), axis=1
            )


def combine_body(chosen, returned, out):
    out[...] = dot(chosen[...], returned[...]).astype(BF16)


def whole(shape):
    return pl.BlockSpec(shape, lambda *_: (0,) * len(shape))


def exchange(value):
    return lax.all_to_all(value, BOTH, 0, 0, tiled=True)


def spread_codebook(codebook):
    book = codebook.reshape(CENTROIDS, CHUNKS, FEATS).transpose(1, 0, 2)
    own = jnp.arange(16)[:, None] == jnp.arange(FEATS)[None, :] // SUBDIM
    spread = jnp.where(own[None, None], book[:, :, None, :], 0.0)
    spread = spread.reshape(CHUNKS, ENTRIES, FEATS)
    high = lax.reduce_precision(spread, 8, 7)
    return high.astype(BF16), (spread - high).astype(BF16)


def shards(queries, probes, targets, passage_codes, codebook):
    devices = lax.axis_size("corpus") * lax.axis_size("query")
    count = queries.shape[0]
    own_lists = passage_codes.shape[0] // lax.axis_size("query")
    per_device = own_lists * CAP
    slots = devices * per_device
    list_rows = devices * CAP
    probes_t = probes.T
    big = pltpu.CompilerParams(
        dimension_semantics=("arbitrary",), vmem_limit_bytes=58 * 1024 * 1024
    )

    sending = pl.pallas_call(
        dispatch_body,
        out_shape=jax.ShapeDtypeStruct((slots, D), BF16),
        grid=(8,),
        in_specs=[whole((PROBES, count)), whole((count, D))],
        out_specs=pl.BlockSpec((slots // 8, D), lambda b: (b, 0)),
        name="dispatch",
    )(probes_t, queries)
    got = exchange(sending)

    chosen, masks, notes = pl.pallas_call(
        home_body,
        out_shape=(
            jax.ShapeDtypeStruct((count, slots), BF16),
            jax.ShapeDtypeStruct((per_device, devices, count), BF16),
            jax.ShapeDtypeStruct((devices, 128), F32),
        ),
        name="home",
    )(probes_t, probes, jnp.tile(targets, (1, 128 // TARGETS)))
    high, low = spread_codebook(codebook)
    offset = (lax.axis_index("query") * own_lists).astype(jnp.int32).reshape(1)
    codes_spec = pl.BlockSpec((1, SUBSPACES, PASSAGES), lambda i, off: (off[0] + i, 0, 0))
    exps_spec = pl.BlockSpec((1, list_rows, PASSAGES), lambda i, off: (i, 0, 0))
    table_spec = whole((CHUNKS, ENTRIES, FEATS))

    exps, stats = pl.pallas_call(
        score_body,
        out_shape=(
            jax.ShapeDtypeStruct((own_lists, list_rows, PASSAGES), F32),
            jax.ShapeDtypeStruct((devices, 128), F32),
        ),
        grid_spec=pltpu.PrefetchScalarGridSpec(
            num_scalar_prefetch=1,
            grid=(own_lists,),
            in_specs=[whole((slots, D)), table_spec, table_spec, codes_spec],
            out_specs=[exps_spec, whole((devices, 128))],
            scratch_shapes=[
                pltpu.VMEM((WIDTH // 128, slots, 128), F32),
                pltpu.VMEM((WIDTH, PASSAGES), BF16),
            ],
        ),
        compiler_params=big,
        name="score",
    )(offset, got, high, low, passage_codes)

    message = pl.pallas_call(
        weight_body,
        out_shape=jax.ShapeDtypeStruct((devices, 256), F32),
        name="weigh",
    )(exchange(stats), masks, notes)

    partial_value, book = pl.pallas_call(
        grad_body,
        out_shape=(
            jax.ShapeDtypeStruct((slots, D), BF16),
            jax.ShapeDtypeStruct((CENTROIDS, D), F32),
        ),
        grid_spec=pltpu.PrefetchScalarGridSpec(
            num_scalar_prefetch=1,
            grid=(own_lists,),
            in_specs=[
                exps_spec,
                whole((devices, 256)),
                codes_spec,
                whole((slots, D)),
                table_spec,
                table_spec,
            ],
            out_specs=[whole((slots, D)), whole((CENTROIDS, D))],
            scratch_shapes=[
                pltpu.VMEM((WIDTH // 128, slots, 128), F32),
                pltpu.VMEM((WIDTH, PASSAGES), BF16),
            ],
        ),
        compiler_params=big,
        name="grad",
    )(offset, exps, exchange(message), passage_codes, got, high, low)

    book_parts = exchange(book.reshape(devices, -1))
    own_sum = jnp.sum(book_parts, axis=0, keepdims=True)
    book_sum = exchange(jnp.broadcast_to(own_sum, book_parts.shape)).reshape(CENTROIDS, D)
    normed = book_sum * lax.rsqrt(jnp.mean(book_sum * book_sum) + EPSILON)

    grad_queries = pl.pallas_call(
        combine_body,
        out_shape=jax.ShapeDtypeStruct((count, D), BF16),
        grid=(3,),
        in_specs=[whole((count, slots)), pl.BlockSpec((slots, D // 3), lambda b: (0, b))],
        out_specs=pl.BlockSpec((count, D // 3), lambda b: (0, b)),
        name="combine",
    )(chosen, exchange(partial_value))
    return grad_queries, normed


def solution(mesh):
    placed = (
        P(BOTH, None),
        P(BOTH, None),
        P(BOTH, None),
        P("corpus", None, None),
        P(),
    )
    return jax.shard_map(
        shards,
        mesh=mesh,
        in_specs=placed,
        out_specs=(P(BOTH, None), P()),
        check_vma=False,
    )
```

```python
import jax
import jax.numpy as jnp
from jax import lax
from jax.experimental import pallas as pl
from jax.experimental.pallas import tpu as pltpu
from jax.sharding import PartitionSpec as P


D = 768
SUBSPACES = 96
CENTROIDS = 16
SUBDIM = 8
PASSAGES = 1024
PROBES = 4
TARGETS = 8
CAP = 2
EPSILON = 1e-06

BOTH = ("corpus", "query")
CHUNKS = 6
FEATS = 128
ENTRIES = 256
WIDTH = SUBSPACES * CENTROIDS
OWN = 8
SLOTS = OWN * CAP
F32 = jnp.float32
BF16 = jnp.bfloat16


def dot(a, b, dims=((1,), (0,))):
    return lax.dot_general(a, b, (dims, ((), ())), preferred_element_type=F32)


def iota(shape, axis):
    return lax.broadcasted_iota(jnp.int32, shape, axis)


def ones_where(mask):
    return jnp.where(mask, 1.0, 0.0).astype(BF16)


def split_two(value):
    high = value.astype(BF16)
    return high, (value - high.astype(F32)).astype(BF16)


def names_list(probe_rows, lists):
    found = probe_rows[0:1, :] == lists
    for p in range(1, PROBES):
        found = found | (probe_rows[p : p + 1, :] == lists)
    return found


def dispatch_body(probes_t, queries, sending):
    count = queries.shape[0]
    rows = sending.shape[0] // CAP
    lists = iota((rows, count), 0) + pl.program_id(0) * rows
    found = names_list(probes_t[...], lists)
    before = ones_where(iota((count, count), 0) < iota((count, count), 1))
    rank = dot(ones_where(found), before)
    chosen = [
        jnp.where(found & (rank == float(r)), 1.0, 0.0).reshape(rows // OWN, 1, OWN, count)
        for r in range(CAP)
    ]
    chosen = jnp.concatenate(chosen, axis=1).reshape(rows * CAP, count).astype(BF16)
    sending[...] = dot(chosen, queries[...]).astype(BF16)


def home_body(probes_t, probes, targets_wide, chosen_out, masks_out, notes_out):
    count = probes.shape[0]
    slots = chosen_out.shape[1]
    devices = notes_out.shape[0]
    block = 512
    after = ones_where(iota((count, count), 0) > iota((count, count), 1))
    for b in range(slots // block):
        slot = iota((count, block), 1) + b * block
        lists = (slot // SLOTS) * OWN + (slot & (OWN - 1))
        found = probes[:, 0:1] == lists
        for p in range(1, PROBES):
            found = found | (probes[:, p : p + 1] == lists)
        rank = dot(after, ones_where(found))
        wanted = ((slot // OWN) & 1).astype(F32)
        chosen_out[:, b * block : (b + 1) * block] = ones_where(found & (rank == wanted))
    wide = targets_wide[...]
    spot = wide & (PASSAGES - 1)
    column = wide // PASSAGES
    in_list = jnp.broadcast_to(probes[:, 0:1], wide.shape)
    for p in range(1, PROBES):
        in_list = jnp.where(column == p, probes[:, p : p + 1], in_list)
    parts = jnp.concatenate(
        [in_list >> 5, in_list & 31, spot >> 5, spot & 31], axis=1
    ).astype(F32).astype(BF16)
    before = ones_where(iota((count, count), 0) < iota((count, count), 1))
    lane = iota((devices, 128), 1)
    gathered = jnp.zeros((devices, 4 * 128), F32)
    lane_wide = iota((devices, 4 * 128), 1) & 127
    for i in range(OWN):
        found = names_list(probes_t[...], iota((devices, count), 0) * OWN + i)
        rank = dot(ones_where(found), before)
        for r in range(CAP):
            mask = ones_where(found & (rank == float(r)))
            masks_out[r * OWN + i] = mask
            here = dot(mask, parts)
            gathered = jnp.where(lane_wide // TARGETS == r * OWN + i, here, gathered)
    got_list = gathered[:, 0:128] * 32.0 + gathered[:, 128:256]
    got_spot = gathered[:, 256:384] * 32.0 + gathered[:, 384:512]
    own_list = iota((devices, 128), 0) * OWN + ((lane // TARGETS) & (OWN - 1))
    notes_out[...] = jnp.where(got_list == own_list.astype(F32), got_spot + 1.0, 0.0)


def one_hot_body(offset, codes, one_hot):
    for c in range(CHUNKS):
        part = codes[0, c * 16 : (c + 1) * 16, :].astype(F32).astype(BF16)
        for k in range(CENTROIDS):
            at = c * ENTRIES + k * 16
            one_hot[0, at : at + 16, :] = jnp.where(
                part == jnp.asarray(k, BF16), jnp.asarray(1, BF16), jnp.asarray(0, BF16)
            )


def score_body(got, high, low, one_hot, masks, exps, stats, table):
    i = pl.program_id(0)
    half = stats.shape[0]

    @pl.when(i == 0)
    def _():
        stats[...] = jnp.zeros_like(stats)
        for c in range(CHUNKS):
            rows = got[:, c * FEATS : (c + 1) * FEATS]
            twice = jnp.concatenate([rows, rows], axis=1)
            weights = jnp.concatenate([high[c], low[c]], axis=1)
            looked = dot(twice, weights, ((1,), (1,)))
            table[2 * c] = looked[:, 0:128]
            table[2 * c + 1] = looked[:, 128:256]

    rows = jnp.concatenate(
        [
            jnp.concatenate(
                [
                    table[j, pl.ds(r * OWN + i, half, stride=SLOTS), :].astype(BF16)
                    for j in range(WIDTH // 128)
                ],
                axis=1,
            )
            for r in range(CAP)
        ],
        axis=0,
    )
    scores = dot(rows, one_hot[0])
    top = jnp.max(scores, axis=1, keepdims=True)
    exp_scores = jnp.exp(scores - top)
    total = jnp.sum(exp_scores, axis=1, keepdims=True)
    exps[0] = exp_scores
    lane = iota(stats.shape, 1)
    held = stats[...]
    for r in range(CAP):
        at = r * OWN + i
        held = jnp.where(lane == at, top[r * half : (r + 1) * half], held)
        held = jnp.where(lane == SLOTS + at, total[r * half : (r + 1) * half], held)
    stats[...] = held


def weight_body(stats, masks, notes, message):
    devices, count = masks.shape[1:]
    low = -3.0e38
    peak = jnp.full((devices, count), low, F32)
    for s in range(SLOTS):
        peak = jnp.maximum(peak, jnp.where(masks[s] > 0, stats[:, s : s + 1], low))
    peak = jnp.max(peak, axis=0, keepdims=True)
    denom = jnp.zeros((devices, count), F32)
    for s in range(SLOTS):
        part = jnp.exp(stats[:, s : s + 1] - peak) * stats[:, SLOTS + s : SLOTS + 1 + s]
        denom = denom + jnp.where(masks[s] > 0, part, 0.0)
    denom = jnp.sum(denom, axis=0, keepdims=True)
    lane = iota((devices, 128), 1)
    held = jnp.zeros((devices, 128), F32)
    for s in range(SLOTS):
        part = jnp.exp(stats[:, s : s + 1] - peak) / denom
        part = jnp.sum(jnp.where(masks[s] > 0, part, 0.0), axis=1, keepdims=True)
        held = jnp.where(lane == s, part, held)
    message[...] = jnp.stack([held, notes[...]], axis=1).reshape(message.shape)


def grad_body(exps, message, one_hot, got, high, low, part_out, book_out, hist):
    i = pl.program_id(0)
    half = message.shape[0] // 2
    lane = iota((half, 128), 1)
    weights = message[pl.ds(0, half, stride=2), :]
    turned = pltpu.roll(message[pl.ds(1, half, stride=2), :], (128 - TARGETS * i) % 128, 1)
    place = iota((half, PASSAGES), 1).astype(F32)
    grads = []
    for r in range(CAP):
        scale = jnp.sum(jnp.where(lane == r * OWN + i, weights, 0.0), axis=1, keepdims=True)
        teacher = jnp.zeros((half, PASSAGES), F32)
        for t in range(TARGETS):
            at = r * OWN * TARGETS + t
            weight = 2.0 * (TARGETS - t) / (TARGETS * (TARGETS + 1.0))
            teacher = jnp.where(place == turned[:, at : at + 1] - 1.0, weight, teacher)
        student = exps[0, r * half : (r + 1) * half, :] * scale
        grads.append((student - teacher).astype(BF16))
    grads = jnp.concatenate(grads, axis=0)
    found = dot(grads, one_hot[0], ((1,), (1,)))
    for r in range(CAP):
        for j in range(WIDTH // 128):
            hist[j, pl.ds(r * OWN + i, half, stride=SLOTS), :] = found[
                r * half : (r + 1) * half, j * 128 : (j + 1) * 128
            ]

    @pl.when(i == pl.num_programs(0) - 1)
    def _():
        keep = iota((ENTRIES, FEATS), 0) % 16 == iota((ENTRIES, FEATS), 1) // SUBDIM
        for c in range(CHUNKS):
            h_high, h_low = split_two(jnp.concatenate([hist[2 * c], hist[2 * c + 1]], axis=1))
            both = jnp.concatenate([high[c], low[c]], axis=1)
            wide = dot(h_high, both)
            part = wide[:, 0:FEATS] + wide[:, FEATS:] + dot(h_low, high[c])
            part_out[:, c * FEATS : (c + 1) * FEATS] = part.astype(BF16)
            book = dot(got[:, c * FEATS : (c + 1) * FEATS], h_high, ((0,), (0,)))
            book = jnp.where(keep, book.T, 0.0)
            book_out[:, c * FEATS : (c + 1) * FEATS] = jnp.sum(
                book.reshape(CENTROIDS, 16, FEATS), axis=1
            )


def norm_body(raw, normed):
    value = raw[...]
    mean = jnp.sum(value * value, keepdims=True) / (CENTROIDS * D)
    normed[...] = value * lax.rsqrt(mean + EPSILON)


def combine_body(chosen, returned, out):
    out[...] = dot(chosen[...], returned[...]).astype(BF16)


def whole(shape):
    return pl.BlockSpec(shape, lambda *_: (0,) * len(shape))


def exchange(value):
    return lax.all_to_all(value, BOTH, 0, 0, tiled=True)


def sum_everywhere(value, devices):
    step = 1
    while step < devices:
        other = lax.ppermute(value, BOTH, [(d, d ^ step) for d in range(devices)])
        value = value + other
        step *= 2
    return value


def spread_codebook(codebook):
    book = codebook.reshape(CENTROIDS, CHUNKS, FEATS).transpose(1, 0, 2)
    own = jnp.arange(16)[:, None] == jnp.arange(FEATS)[None, :] // SUBDIM
    spread = jnp.where(own[None, None], book[:, :, None, :], 0.0)
    spread = spread.reshape(CHUNKS, ENTRIES, FEATS)
    high = lax.reduce_precision(spread, 8, 7)
    return high.astype(BF16), (spread - high).astype(BF16)


def shards(queries, probes, targets, passage_codes, codebook):
    devices = lax.axis_size("corpus") * lax.axis_size("query")
    count = queries.shape[0]
    slots = devices * SLOTS
    list_rows = devices * CAP
    probes_t = probes.T
    big = pltpu.CompilerParams(
        dimension_semantics=("arbitrary",), vmem_limit_bytes=58 * 1024 * 1024
    )
    square = jax.ShapeDtypeStruct((devices, 128), F32)

    sending = pl.pallas_call(
        dispatch_body,
        out_shape=jax.ShapeDtypeStruct((slots, D), BF16),
        grid=(4,),
        in_specs=[whole((PROBES, count)), whole((count, D))],
        out_specs=pl.BlockSpec((slots // 4, D), lambda b: (b, 0)),
        name="dispatch",
    )(probes_t, queries)
    got = exchange(sending)

    chosen, masks, notes = pl.pallas_call(
        home_body,
        out_shape=(
            jax.ShapeDtypeStruct((count, slots), BF16),
            jax.ShapeDtypeStruct((SLOTS, devices, count), BF16),
            square,
        ),
        name="home",
    )(probes_t, probes, jnp.tile(targets, (1, 128 // TARGETS)))
    high, low = spread_codebook(codebook)
    offset = (lax.axis_index("query") * OWN).astype(jnp.int32).reshape(1)
    one_hot = pl.pallas_call(
        one_hot_body,
        out_shape=jax.ShapeDtypeStruct((OWN, WIDTH, PASSAGES), BF16),
        grid_spec=pltpu.PrefetchScalarGridSpec(
            num_scalar_prefetch=1,
            grid=(OWN,),
            in_specs=[
                pl.BlockSpec((1, SUBSPACES, PASSAGES), lambda i, off: (off[0] + i, 0, 0))
            ],
            out_specs=pl.BlockSpec((1, WIDTH, PASSAGES), lambda i, off: (i, 0, 0)),
        ),
        name="one_hot",
    )(offset, passage_codes)

    by_list = lambda *shape: pl.BlockSpec((1,) + shape, lambda i: (i, 0, 0))
    exps_spec = by_list(list_rows, PASSAGES)
    one_hot_spec = by_list(WIDTH, PASSAGES)
    table_spec = whole((CHUNKS, ENTRIES, FEATS))
    per_list = jax.ShapeDtypeStruct((OWN, list_rows, PASSAGES), F32)
    scratch = [pltpu.VMEM((WIDTH // 128, slots, 128), F32)]

    exps, stats = pl.pallas_call(
        score_body,
        out_shape=(per_list, square),
        grid=(OWN,),
        in_specs=[
            whole((slots, D)),
            table_spec,
            table_spec,
            one_hot_spec,
            pl.BlockSpec(memory_space=pl.ANY),
        ],
        out_specs=[exps_spec, whole(square.shape)],
        scratch_shapes=scratch,
        compiler_params=big,
        name="score",
    )(got, high, low, one_hot, masks)

    message = pl.pallas_call(
        weight_body, out_shape=jax.ShapeDtypeStruct((2 * devices, 128), F32), name="weigh"
    )(exchange(stats), masks, notes)

    partial_value, book = pl.pallas_call(
        grad_body,
        out_shape=(
            jax.ShapeDtypeStruct((slots, D), BF16),
            jax.ShapeDtypeStruct((CENTROIDS, D), F32),
        ),
        grid=(OWN,),
        in_specs=[
            exps_spec,
            whole((2 * devices, 128)),
            one_hot_spec,
            whole((slots, D)),
            table_spec,
            table_spec,
        ],
        out_specs=[whole((slots, D)), whole((CENTROIDS, D))],
        scratch_shapes=scratch,
        compiler_params=big,
        name="grad",
    )(exps, exchange(message), one_hot, got, high, low)

    normed = pl.pallas_call(
        norm_body, out_shape=jax.ShapeDtypeStruct((CENTROIDS, D), F32), name="book_norm"
    )(sum_everywhere(book, devices))

    grad_queries = pl.pallas_call(
        combine_body,
        out_shape=jax.ShapeDtypeStruct((count, D), BF16),
        grid=(3,),
        in_specs=[whole((count, slots)), pl.BlockSpec((slots, D // 3), lambda b: (0, b))],
        out_specs=pl.BlockSpec((count, D // 3), lambda b: (0, b)),
        name="combine",
    )(chosen, exchange(partial_value))
    return grad_queries, normed


def solution(mesh):
    placed = (
        P(BOTH, None),
        P(BOTH, None),
        P(BOTH, None),
        P("corpus", None, None),
        P(),
    )

    return jax.shard_map(
        shards,
        mesh=mesh,
        in_specs=placed,
        out_specs=(P(BOTH, None), P()),
        check_vma=False,
    )
```

```python
import jax
import jax.numpy as jnp
from jax import lax
from jax.experimental import pallas as pl
from jax.experimental.pallas import tpu as pltpu
from jax.sharding import PartitionSpec as P


D = 768
SUBSPACES = 96
CENTROIDS = 16
SUBDIM = 8
PASSAGES = 1024
PROBES = 4
TARGETS = 8
CAP = 2
EPSILON = 1e-06

BOTH = ("corpus", "query")
CHUNKS = 6
FEATS = 128
ENTRIES = 256
WIDTH = SUBSPACES * CENTROIDS
OWN = 8
SLOTS = OWN * CAP
BOOK_ROWS = 8
F32 = jnp.float32
BF16 = jnp.bfloat16


def dot(a, b, dims=((1,), (0,))):
    return lax.dot_general(a, b, (dims, ((), ())), preferred_element_type=F32)


def iota(shape, axis):
    return lax.broadcasted_iota(jnp.int32, shape, axis)


def ones_where(mask):
    return jnp.where(mask, 1.0, 0.0).astype(BF16)


def split_two(value):
    high = value.astype(BF16)
    return high, (value - high.astype(F32)).astype(BF16)


def names_list(probe_rows, lists):
    found = probe_rows[0:1, :] == lists
    for p in range(1, PROBES):
        found = found | (probe_rows[p : p + 1, :] == lists)
    return found


def dispatch_body(probes_t, queries, sending):
    count = queries.shape[0]
    rows = sending.shape[0] // CAP
    lists = iota((rows, count), 0) + pl.program_id(0) * rows
    found = names_list(probes_t[...], lists)
    before = ones_where(iota((count, count), 0) < iota((count, count), 1))
    rank = dot(ones_where(found), before)
    chosen = [
        jnp.where(found & (rank == float(r)), 1.0, 0.0).reshape(rows // OWN, 1, OWN, count)
        for r in range(CAP)
    ]
    chosen = jnp.concatenate(chosen, axis=1).reshape(rows * CAP, count).astype(BF16)
    sending[...] = dot(chosen, queries[...]).astype(BF16)


def home_body(probes_t, probes, targets_wide, chosen_out, masks_out, notes_out):
    count = probes.shape[0]
    slots = chosen_out.shape[1]
    devices = notes_out.shape[0]
    block = 512
    after = ones_where(iota((count, count), 0) > iota((count, count), 1))
    for b in range(slots // block):
        slot = iota((count, block), 1) + b * block
        lists = (slot // SLOTS) * OWN + (slot & (OWN - 1))
        found = probes[:, 0:1] == lists
        for p in range(1, PROBES):
            found = found | (probes[:, p : p + 1] == lists)
        rank = dot(after, ones_where(found))
        wanted = ((slot // OWN) & 1).astype(F32)
        chosen_out[:, b * block : (b + 1) * block] = ones_where(found & (rank == wanted))
    wide = targets_wide[...]
    spot = wide & (PASSAGES - 1)
    column = wide // PASSAGES
    in_list = jnp.broadcast_to(probes[:, 0:1], wide.shape)
    for p in range(1, PROBES):
        in_list = jnp.where(column == p, probes[:, p : p + 1], in_list)
    parts = jnp.concatenate(
        [in_list >> 5, in_list & 31, spot >> 5, spot & 31], axis=1
    ).astype(F32).astype(BF16)
    before = ones_where(iota((count, count), 0) < iota((count, count), 1))
    lane = iota((devices, 128), 1)
    gathered = jnp.zeros((devices, 4 * 128), F32)
    lane_wide = iota((devices, 4 * 128), 1) & 127
    for i in range(OWN):
        found = names_list(probes_t[...], iota((devices, count), 0) * OWN + i)
        rank = dot(ones_where(found), before)
        for r in range(CAP):
            mask = ones_where(found & (rank == float(r)))
            masks_out[r * OWN + i] = mask
            here = dot(mask, parts)
            gathered = jnp.where(lane_wide // TARGETS == r * OWN + i, here, gathered)
    got_list = gathered[:, 0:128] * 32.0 + gathered[:, 128:256]
    got_spot = gathered[:, 256:384] * 32.0 + gathered[:, 384:512]
    own_list = iota((devices, 128), 0) * OWN + ((lane // TARGETS) & (OWN - 1))
    notes_out[...] = jnp.where(got_list == own_list.astype(F32), got_spot + 1.0, 0.0)


def fill_one_hot(codes, one_hot):
    for c in range(CHUNKS):
        part = codes[0, c * 16 : (c + 1) * 16, :].astype(F32).astype(BF16)
        for k in range(CENTROIDS):
            at = c * ENTRIES + k * 16
            one_hot[at : at + 16, :] = jnp.where(
                part == jnp.asarray(k, BF16), jnp.asarray(1, BF16), jnp.asarray(0, BF16)
            )


def score_body(
    offset, got, high, low, first, odd, even, exps, stats, table, hot_a, hot_b, held_a, held_b
):
    s = pl.program_id(0)
    half = stats.shape[0]

    def score(i, hot, held):
        rows = jnp.concatenate(
            [
                jnp.concatenate(
                    [
                        table[j, pl.ds(r * OWN + i, half, stride=SLOTS), :].astype(BF16)
                        for j in range(WIDTH // 128)
                    ],
                    axis=1,
                )
                for r in range(CAP)
            ],
            axis=0,
        )
        held[...] = dot(rows, hot[...])

    def soften(i, held, place):
        scores = held[...]
        top = jnp.max(scores, axis=1, keepdims=True)
        exp_scores = jnp.exp(scores - top)
        total = jnp.sum(exp_scores, axis=1, keepdims=True)
        exps[place] = exp_scores
        lane = iota(stats.shape, 1)
        kept = stats[...]
        for r in range(CAP):
            at = r * OWN + i
            kept = jnp.where(lane == at, top[r * half : (r + 1) * half], kept)
            kept = jnp.where(lane == SLOTS + at, total[r * half : (r + 1) * half], kept)
        stats[...] = kept

    last = pl.num_programs(0) - 1

    @pl.when(s == 0)
    def _():
        stats[...] = jnp.zeros_like(stats)
        held_b[...] = jnp.zeros_like(held_b)
        fill_one_hot(first, hot_a)
        for c in range(CHUNKS):
            rows = got[:, c * FEATS : (c + 1) * FEATS]
            twice = jnp.concatenate([rows, rows], axis=1)
            weights = jnp.concatenate([high[c], low[c]], axis=1)
            looked = dot(twice, weights, ((1,), (1,)))
            table[2 * c] = looked[:, 0:128]
            table[2 * c + 1] = looked[:, 128:256]

    @pl.when(s < last)
    def _():
        score(2 * s, hot_a, held_a)
        fill_one_hot(odd, hot_b)
        soften(2 * s - 1, held_b, 0)
        score(2 * s + 1, hot_b, held_b)
        fill_one_hot(even, hot_a)
        soften(2 * s, held_a, 1)

    @pl.when(s == last)
    def _():
        soften(2 * s - 1, held_b, 0)
        exps[1] = jnp.zeros(exps.shape[1:], F32)


def weight_body(stats, masks, notes, message):
    devices, count = masks.shape[1:]
    low = -3.0e38
    peak = jnp.full((devices, count), low, F32)
    for s in range(SLOTS):
        peak = jnp.maximum(peak, jnp.where(masks[s] > 0, stats[:, s : s + 1], low))
    peak = jnp.max(peak, axis=0, keepdims=True)
    denom = jnp.zeros((devices, count), F32)
    for s in range(SLOTS):
        part = jnp.exp(stats[:, s : s + 1] - peak) * stats[:, SLOTS + s : SLOTS + 1 + s]
        denom = denom + jnp.where(masks[s] > 0, part, 0.0)
    denom = jnp.sum(denom, axis=0, keepdims=True)
    lane = iota((devices, 128), 1)
    held = jnp.zeros((devices, 128), F32)
    for s in range(SLOTS):
        part = jnp.exp(stats[:, s : s + 1] - peak) / denom
        part = jnp.sum(jnp.where(masks[s] > 0, part, 0.0), axis=1, keepdims=True)
        held = jnp.where(lane == s, part, held)
    message[...] = jnp.stack([held, notes[...]], axis=1).reshape(message.shape)


def grad_body(
    offset, message, got, high, low, exps_first, exps_odd, exps_even, first, odd, even,
    out, hist, hot_a, hot_b, grads_a, grads_b,
):
    s = pl.program_id(0)
    half = message.shape[0] // 2
    place = iota((half, PASSAGES), 1).astype(F32)

    def prepare(i, exps, codes, hot, grads):
        lane = iota((half, 128), 1)
        weights = message[pl.ds(0, half, stride=2), :]
        notes = message[pl.ds(1, half, stride=2), :]
        turned = pltpu.roll(notes, (128 - TARGETS * i) % 128, 1)
        for r in range(CAP):
            scale = jnp.sum(jnp.where(lane == r * OWN + i, weights, 0.0), axis=1, keepdims=True)
            teacher = jnp.zeros((half, PASSAGES), F32)
            for t in range(TARGETS):
                at = r * OWN * TARGETS + t
                weight = 2.0 * (TARGETS - t) / (TARGETS * (TARGETS + 1.0))
                teacher = jnp.where(place == turned[:, at : at + 1] - 1.0, weight, teacher)
            student = exps[0, r * half : (r + 1) * half, :] * scale
            grads[r * half : (r + 1) * half, :] = (student - teacher).astype(BF16)
        fill_one_hot(codes, hot)

    def count(i, hot, grads):
        found = dot(grads[...], hot[...], ((1,), (1,)))
        for r in range(CAP):
            for j in range(WIDTH // 128):
                hist[j, pl.ds(r * OWN + i, half, stride=SLOTS), :] = found[
                    r * half : (r + 1) * half, j * 128 : (j + 1) * 128
                ]

    @pl.when(s == 0)
    def _():
        prepare(0, exps_first, first, hot_a, grads_a)

    count(2 * s, hot_a, grads_a)
    prepare(2 * s + 1, exps_odd, odd, hot_b, grads_b)
    count(2 * s + 1, hot_b, grads_b)
    prepare(jnp.minimum(2 * s + 2, OWN - 1), exps_even, even, hot_a, grads_a)

    @pl.when(s == pl.num_programs(0) - 1)
    def _():
        devices = out.shape[0]
        keep = iota((ENTRIES, FEATS), 0) % 16 == iota((ENTRIES, FEATS), 1) // SUBDIM
        top = CHUNKS * SLOTS
        out[CHUNKS * CENTROIDS :, top:, :] = jnp.zeros(
            (devices - CHUNKS * CENTROIDS, BOOK_ROWS, 128), BF16
        )
        for c in range(CHUNKS):
            h_high, h_low = split_two(jnp.concatenate([hist[2 * c], hist[2 * c + 1]], axis=1))
            both = jnp.concatenate([high[c], low[c]], axis=1)
            wide = dot(h_high, both)
            part = wide[:, 0:FEATS] + wide[:, FEATS:] + dot(h_low, high[c])
            out[:, c * SLOTS : (c + 1) * SLOTS, :] = part.reshape(devices, SLOTS, FEATS).astype(
                BF16
            )
            book = dot(got[:, c * FEATS : (c + 1) * FEATS], h_high, ((0,), (0,)))
            book = jnp.where(keep, book.T, 0.0)
            book = jnp.sum(book.reshape(CENTROIDS, 16, FEATS), axis=1)
            b_high = book.astype(BF16)
            b_rest = book - b_high.astype(F32)
            b_mid = b_rest.astype(BF16)
            b_low = b_rest - b_mid.astype(F32)
            row = iota((CENTROIDS, BOOK_ROWS, FEATS), 1)
            parts = jnp.where(row == 0, b_high.astype(F32)[:, None, :], 0.0)
            parts = jnp.where(row == 1, b_mid.astype(F32)[:, None, :], parts)
            parts = jnp.where(row == 2, b_low[:, None, :], parts)
            out[c * CENTROIDS : (c + 1) * CENTROIDS, top:, :] = parts.astype(BF16)


def book_body(returned, total):
    parts = returned[...].astype(F32)
    total[...] = jnp.broadcast_to(
        jnp.sum(jnp.sum(parts, axis=0), axis=0, keepdims=True), total.shape
    )


def norm_body(rows, normed):
    value = rows[0 : CHUNKS * CENTROIDS, :]
    mean = jnp.sum(value * value, keepdims=True) / (CENTROIDS * D)
    value = value * lax.rsqrt(mean + EPSILON)
    for c in range(CHUNKS):
        normed[:, c * FEATS : (c + 1) * FEATS] = value[c * CENTROIDS : (c + 1) * CENTROIDS]


def combine_body(chosen, returned, out):
    devices = returned.shape[0]
    for c in range(CHUNKS):
        rows = returned[:, c * SLOTS : (c + 1) * SLOTS, :].reshape(devices * SLOTS, FEATS)
        out[:, c * FEATS : (c + 1) * FEATS] = dot(chosen[...], rows).astype(BF16)


def whole(shape):
    return pl.BlockSpec(shape, lambda *_: (0,) * len(shape))


def exchange(value):
    return lax.all_to_all(value, BOTH, 0, 0, tiled=True)


def spread_codebook(codebook):
    book = codebook.reshape(CENTROIDS, CHUNKS, FEATS).transpose(1, 0, 2)
    own = jnp.arange(16)[:, None] == jnp.arange(FEATS)[None, :] // SUBDIM
    spread = jnp.where(own[None, None], book[:, :, None, :], 0.0)
    spread = spread.reshape(CHUNKS, ENTRIES, FEATS)
    high = lax.reduce_precision(spread, 8, 7)
    return high.astype(BF16), (spread - high).astype(BF16)


def shards(queries, probes, targets, passage_codes, codebook):
    devices = lax.axis_size("corpus") * lax.axis_size("query")
    count = queries.shape[0]
    slots = devices * SLOTS
    list_rows = devices * CAP
    probes_t = probes.T
    big = pltpu.CompilerParams(
        dimension_semantics=("arbitrary",), vmem_limit_bytes=58 * 1024 * 1024
    )
    square = jax.ShapeDtypeStruct((devices, 128), F32)

    sending = pl.pallas_call(
        dispatch_body,
        out_shape=jax.ShapeDtypeStruct((slots, D), BF16),
        grid=(4,),
        in_specs=[whole((PROBES, count)), whole((count, D))],
        out_specs=pl.BlockSpec((slots // 4, D), lambda b: (b, 0)),
        name="dispatch",
    )(probes_t, queries)
    got = exchange(sending)

    chosen, masks, notes = pl.pallas_call(
        home_body,
        out_shape=(
            jax.ShapeDtypeStruct((count, slots), BF16),
            jax.ShapeDtypeStruct((SLOTS, devices, count), BF16),
            square,
        ),
        name="home",
    )(probes_t, probes, jnp.tile(targets, (1, 128 // TARGETS)))
    high, low = spread_codebook(codebook)
    offset = (lax.axis_index("query") * OWN).astype(jnp.int32).reshape(1)

    def code_of(index):
        return pl.BlockSpec(
            (1, SUBSPACES, PASSAGES), lambda s, off: (off[0] + index(s), 0, 0)
        )

    code_specs = [
        code_of(lambda s: 0),
        code_of(lambda s: jnp.minimum(2 * s + 1, OWN - 1)),
        code_of(lambda s: jnp.minimum(2 * s + 2, OWN - 1)),
    ]
    table_spec = whole((CHUNKS, ENTRIES, FEATS))
    table = pltpu.VMEM((WIDTH // 128, slots, 128), F32)
    hot = pltpu.VMEM((WIDTH, PASSAGES), BF16)
    codes = (passage_codes,) * 3

    exps, stats = pl.pallas_call(
        score_body,
        out_shape=(jax.ShapeDtypeStruct((OWN + 2, list_rows, PASSAGES), F32), square),
        grid_spec=pltpu.PrefetchScalarGridSpec(
            num_scalar_prefetch=1,
            grid=(OWN // 2 + 1,),
            in_specs=[whole((slots, D)), table_spec, table_spec] + code_specs,
            out_specs=[
                pl.BlockSpec((2, list_rows, PASSAGES), lambda s, off: (s, 0, 0)),
                whole(square.shape),
            ],
            scratch_shapes=[table, hot, hot] + [pltpu.VMEM((list_rows, PASSAGES), F32)] * 2,
        ),
        compiler_params=big,
        name="score",
    )(offset, got, high, low, *codes)

    message = pl.pallas_call(
        weight_body, out_shape=jax.ShapeDtypeStruct((2 * devices, 128), F32), name="weigh"
    )(exchange(stats), masks, notes)

    def exps_of(index):
        return pl.BlockSpec((1, list_rows, PASSAGES), lambda s, off: (index(s), 0, 0))

    result = pl.pallas_call(
        grad_body,
        out_shape=jax.ShapeDtypeStruct((devices, CHUNKS * SLOTS + BOOK_ROWS, FEATS), BF16),
        grid_spec=pltpu.PrefetchScalarGridSpec(
            num_scalar_prefetch=1,
            grid=(OWN // 2,),
            in_specs=[
                whole((2 * devices, 128)),
                whole((slots, D)),
                table_spec,
                table_spec,
                exps_of(lambda s: 1),
                exps_of(lambda s: 2 * s + 2),
                exps_of(lambda s: jnp.minimum(2 * s + 3, OWN)),
            ]
            + code_specs,
            out_specs=whole((devices, CHUNKS * SLOTS + BOOK_ROWS, FEATS)),
            scratch_shapes=[table, hot, hot] + [pltpu.VMEM((list_rows, PASSAGES), BF16)] * 2,
        ),
        compiler_params=big,
        name="grad",
    )(offset, exchange(message), got, high, low, exps, exps, exps, *codes)

    returned = exchange(result)
    book_spec = pl.BlockSpec(
        (devices, BOOK_ROWS, FEATS), lambda b: (0, CHUNKS * SLOTS // BOOK_ROWS, 0)
    )
    book_sum = pl.pallas_call(
        book_body,
        out_shape=square,
        grid=(1,),
        in_specs=[book_spec],
        out_specs=whole(square.shape),
        name="book_sum",
    )(returned)
    normed = pl.pallas_call(
        norm_body, out_shape=jax.ShapeDtypeStruct((CENTROIDS, D), F32), name="book_norm"
    )(exchange(book_sum))
    grad_queries = pl.pallas_call(
        combine_body,
        out_shape=jax.ShapeDtypeStruct((count, D), BF16),
        grid=(1,),
        in_specs=[
            whole((count, slots)),
            pl.BlockSpec((devices, CHUNKS * SLOTS, FEATS), lambda b: (0, 0, 0)),
        ],
        out_specs=whole((count, D)),
        name="combine",
    )(chosen, returned)
    return grad_queries, normed


def solution(mesh):
    placed = (
        P(BOTH, None),
        P(BOTH, None),
        P(BOTH, None),
        P("corpus", None, None),
        P(),
    )

    return jax.shard_map(
        shards,
        mesh=mesh,
        in_specs=placed,
        out_specs=(P(BOTH, None), P()),
        check_vma=False,
    )
```

```python
import jax
import jax.numpy as jnp
from jax import lax
from jax.experimental import pallas as pl
from jax.experimental.pallas import tpu as pltpu
from jax.sharding import PartitionSpec as P


D = 768
SUBSPACES = 96
CENTROIDS = 16
SUBDIM = 8
PASSAGES = 1024
PROBES = 4
TARGETS = 8
CAP = 2
EPSILON = 1e-06

BOTH = ("corpus", "query")
CHUNKS = 6
FEATS = 128
ENTRIES = 256
WIDTH = SUBSPACES * CENTROIDS
OWN = 8
SLOTS = OWN * CAP
BOOK_ROWS = 8
F32 = jnp.float32
BF16 = jnp.bfloat16


def dot(a, b, dims=((1,), (0,))):
    return lax.dot_general(a, b, (dims, ((), ())), preferred_element_type=F32)


def iota(shape, axis):
    return lax.broadcasted_iota(jnp.int32, shape, axis)


def ones_where(mask):
    return jnp.where(mask, 1.0, 0.0).astype(BF16)


def split_two(value):
    high = value.astype(BF16)
    return high, (value - high.astype(F32)).astype(BF16)


def names_list(probe_rows, lists):
    found = probe_rows[0:1, :] == lists
    for p in range(1, PROBES):
        found = found | (probe_rows[p : p + 1, :] == lists)
    return found


def dispatch_body(probes_t, queries, sending):
    count = queries.shape[0]
    rows = sending.shape[0] // CAP
    lists = iota((rows, count), 0) + pl.program_id(0) * rows
    found = names_list(probes_t[...], lists)
    before = ones_where(iota((count, count), 0) < iota((count, count), 1))
    rank = dot(ones_where(found), before)
    chosen = [
        jnp.where(found & (rank == float(r)), 1.0, 0.0).reshape(rows // OWN, 1, OWN, count)
        for r in range(CAP)
    ]
    chosen = jnp.concatenate(chosen, axis=1).reshape(rows * CAP, count).astype(BF16)
    sending[...] = dot(chosen, queries[...]).astype(BF16)


def home_body(probes_t, probes, targets_wide, chosen_out, masks_out, notes_out):
    count = probes.shape[0]
    slots = chosen_out.shape[1]
    devices = notes_out.shape[0]
    block = 512
    after = ones_where(iota((count, count), 0) > iota((count, count), 1))
    for b in range(slots // block):
        slot = iota((count, block), 1) + b * block
        lists = (slot // SLOTS) * OWN + (slot & (OWN - 1))
        found = probes[:, 0:1] == lists
        for p in range(1, PROBES):
            found = found | (probes[:, p : p + 1] == lists)
        rank = dot(after, ones_where(found))
        wanted = ((slot // OWN) & 1).astype(F32)
        chosen_out[:, b * block : (b + 1) * block] = ones_where(found & (rank == wanted))
    wide = targets_wide[...]
    spot = wide & (PASSAGES - 1)
    column = wide // PASSAGES
    in_list = jnp.broadcast_to(probes[:, 0:1], wide.shape)
    for p in range(1, PROBES):
        in_list = jnp.where(column == p, probes[:, p : p + 1], in_list)
    parts = jnp.concatenate(
        [in_list >> 5, in_list & 31, spot >> 5, spot & 31], axis=1
    ).astype(F32).astype(BF16)
    before = ones_where(iota((count, count), 0) < iota((count, count), 1))
    lane = iota((devices, 128), 1)
    gathered = jnp.zeros((devices, 4 * 128), F32)
    lane_wide = iota((devices, 4 * 128), 1) & 127
    for i in range(OWN):
        found = names_list(probes_t[...], iota((devices, count), 0) * OWN + i)
        rank = dot(ones_where(found), before)
        for r in range(CAP):
            mask = ones_where(found & (rank == float(r)))
            masks_out[r * OWN + i] = mask
            here = dot(mask, parts)
            gathered = jnp.where(lane_wide // TARGETS == r * OWN + i, here, gathered)
    got_list = gathered[:, 0:128] * 32.0 + gathered[:, 128:256]
    got_spot = gathered[:, 256:384] * 32.0 + gathered[:, 384:512]
    own_list = iota((devices, 128), 0) * OWN + ((lane // TARGETS) & (OWN - 1))
    notes_out[...] = jnp.where(got_list == own_list.astype(F32), got_spot + 1.0, 0.0)


def fill_one_hot(codes, one_hot):
    for c in range(CHUNKS):
        part = codes[0, c * 16 : (c + 1) * 16, :].astype(F32).astype(BF16)
        for k in range(CENTROIDS):
            at = c * ENTRIES + k * 16
            one_hot[at : at + 16, :] = jnp.where(
                part == jnp.asarray(k, BF16), jnp.asarray(1, BF16), jnp.asarray(0, BF16)
            )


def score_body(
    offset, got, high, low, notes, first, odd, even,
    exps, message, table, hot_a, hot_b, held_a, held_b, stats,
):
    s = pl.program_id(0)
    half = stats.shape[0]

    def score(i, hot, held):
        rows = jnp.concatenate(
            [
                jnp.concatenate(
                    [
                        table[j, pl.ds(r * OWN + i, half, stride=SLOTS), :].astype(BF16)
                        for j in range(WIDTH // 128)
                    ],
                    axis=1,
                )
                for r in range(CAP)
            ],
            axis=0,
        )
        held[...] = dot(rows, hot[...])

    def soften(i, held, place):
        scores = held[...]
        top = jnp.max(scores, axis=1, keepdims=True)
        exp_scores = jnp.exp(scores - top)
        total = jnp.sum(exp_scores, axis=1, keepdims=True)
        exps[place] = exp_scores
        lane = iota(stats.shape, 1)
        kept = stats[...]
        for r in range(CAP):
            at = r * OWN + i
            kept = jnp.where(lane == at, top[r * half : (r + 1) * half], kept)
            kept = jnp.where(lane == SLOTS + at, total[r * half : (r + 1) * half], kept)
        stats[...] = kept

    last = pl.num_programs(0) - 1

    @pl.when(s == 0)
    def _():
        stats[...] = jnp.zeros_like(stats)
        held_b[...] = jnp.zeros_like(held_b)
        fill_one_hot(first, hot_a)
        for c in range(CHUNKS):
            rows = got[:, c * FEATS : (c + 1) * FEATS]
            twice = jnp.concatenate([rows, rows], axis=1)
            weights = jnp.concatenate([high[c], low[c]], axis=1)
            looked = dot(twice, weights, ((1,), (1,)))
            table[2 * c] = looked[:, 0:128]
            table[2 * c + 1] = looked[:, 128:256]

    @pl.when(s < last)
    def _():
        score(2 * s, hot_a, held_a)
        fill_one_hot(odd, hot_b)
        soften(2 * s - 1, held_b, 0)
        score(2 * s + 1, hot_b, held_b)
        fill_one_hot(even, hot_a)
        soften(2 * s, held_a, 1)

    @pl.when(s == last)
    def _():
        soften(2 * s - 1, held_b, 0)
        exps[1] = jnp.zeros(exps.shape[1:], F32)
        message[...] = jnp.stack([stats[...], notes[...]], axis=1).reshape(message.shape)


def weight_body(stats, masks, weights, ratios):
    devices, count = masks.shape[1:]
    tops = stats[pl.ds(0, devices, stride=2), :]
    low = -3.0e38
    peak = jnp.full((devices, count), low, F32)
    for s in range(SLOTS):
        peak = jnp.maximum(peak, jnp.where(masks[s] > 0, tops[:, s : s + 1], low))
    peak = jnp.max(peak, axis=0, keepdims=True)
    denom = jnp.zeros((devices, count), F32)
    for s in range(SLOTS):
        ratio = jnp.where(masks[s] > 0, jnp.exp(tops[:, s : s + 1] - peak), 0.0)
        ratios[s] = ratio
        denom = denom + ratio * tops[:, SLOTS + s : SLOTS + 1 + s]
    denom = jnp.sum(denom, axis=0, keepdims=True)
    lane = iota((devices, 128), 1)
    held = jnp.zeros((devices, 128), F32)
    for s in range(SLOTS):
        part = jnp.sum(ratios[s] / denom, axis=1, keepdims=True)
        held = jnp.where(lane == s, part, held)
    weights[...] = held


def teacher_body(message, teacher):
    i = pl.program_id(0)
    half = message.shape[0] // 2
    turned = pltpu.roll(message[pl.ds(1, half, stride=2), :], (128 - TARGETS * i) % 128, 1)
    place = iota((half, PASSAGES), 1).astype(F32)
    for r in range(CAP):
        held = jnp.zeros((half, PASSAGES), F32)
        for t in range(TARGETS):
            at = r * OWN * TARGETS + t
            weight = 2.0 * (TARGETS - t) / (TARGETS * (TARGETS + 1.0))
            held = jnp.where(place == turned[:, at : at + 1] - 1.0, weight, held)
        teacher[0, r * half : (r + 1) * half, :] = held


def grad_body(
    offset, weights, got, high, low, exps_first, exps_odd, exps_even,
    teacher_first, teacher_odd, teacher_even, first, odd, even,
    out, hist, hot_a, hot_b, grads_a, grads_b,
):
    s = pl.program_id(0)
    half = weights.shape[0]

    def prepare(i, exps, teacher, codes, hot, grads):
        lane = iota((half, 128), 1)
        for r in range(CAP):
            own = jnp.where(lane == r * OWN + i, weights[...], 0.0)
            scale = jnp.sum(own, axis=1, keepdims=True)
            rows = slice(r * half, (r + 1) * half)
            grads[rows, :] = (exps[0, rows, :] * scale - teacher[0, rows, :]).astype(BF16)
        fill_one_hot(codes, hot)

    def count(i, hot, grads):
        found = dot(grads[...], hot[...], ((1,), (1,)))
        for r in range(CAP):
            for j in range(WIDTH // 128):
                hist[j, pl.ds(r * OWN + i, half, stride=SLOTS), :] = found[
                    r * half : (r + 1) * half, j * 128 : (j + 1) * 128
                ]

    @pl.when(s == 0)
    def _():
        prepare(0, exps_first, teacher_first, first, hot_a, grads_a)

    count(2 * s, hot_a, grads_a)
    prepare(2 * s + 1, exps_odd, teacher_odd, odd, hot_b, grads_b)
    count(2 * s + 1, hot_b, grads_b)
    following = jnp.minimum(2 * s + 2, OWN - 1)
    prepare(following, exps_even, teacher_even, even, hot_a, grads_a)

    @pl.when(s == pl.num_programs(0) - 1)
    def _():
        devices = out.shape[0]
        keep = iota((ENTRIES, FEATS), 0) % 16 == iota((ENTRIES, FEATS), 1) // SUBDIM
        top = CHUNKS * SLOTS
        out[CHUNKS * CENTROIDS :, top:, :] = jnp.zeros(
            (devices - CHUNKS * CENTROIDS, BOOK_ROWS, 128), BF16
        )
        for c in range(CHUNKS):
            h_high, h_low = split_two(jnp.concatenate([hist[2 * c], hist[2 * c + 1]], axis=1))
            both = jnp.concatenate([high[c], low[c]], axis=1)
            wide = dot(h_high, both)
            part = wide[:, 0:FEATS] + wide[:, FEATS:] + dot(h_low, high[c])
            out[:, c * SLOTS : (c + 1) * SLOTS, :] = part.reshape(devices, SLOTS, FEATS).astype(
                BF16
            )
            book = dot(got[:, c * FEATS : (c + 1) * FEATS], h_high, ((0,), (0,)))
            book = jnp.where(keep, book.T, 0.0)
            book = jnp.sum(book.reshape(CENTROIDS, 16, FEATS), axis=1)
            b_high = book.astype(BF16)
            b_rest = book - b_high.astype(F32)
            b_mid = b_rest.astype(BF16)
            b_low = b_rest - b_mid.astype(F32)
            row = iota((CENTROIDS, BOOK_ROWS, FEATS), 1)
            parts = jnp.where(row == 0, b_high.astype(F32)[:, None, :], 0.0)
            parts = jnp.where(row == 1, b_mid.astype(F32)[:, None, :], parts)
            parts = jnp.where(row == 2, b_low[:, None, :], parts)
            out[c * CENTROIDS : (c + 1) * CENTROIDS, top:, :] = parts.astype(BF16)


def book_body(returned, total):
    parts = returned[...].astype(F32)
    total[...] = jnp.broadcast_to(
        jnp.sum(jnp.sum(parts, axis=0), axis=0, keepdims=True), total.shape
    )


def norm_body(rows, normed):
    value = rows[0 : CHUNKS * CENTROIDS, :]
    mean = jnp.sum(value * value, keepdims=True) / (CENTROIDS * D)
    value = value * lax.rsqrt(mean + EPSILON)
    for c in range(CHUNKS):
        normed[:, c * FEATS : (c + 1) * FEATS] = value[c * CENTROIDS : (c + 1) * CENTROIDS]


def combine_body(chosen, returned, out):
    devices = returned.shape[0]
    for c in range(CHUNKS):
        rows = returned[:, c * SLOTS : (c + 1) * SLOTS, :].reshape(devices * SLOTS, FEATS)
        out[:, c * FEATS : (c + 1) * FEATS] = dot(chosen[...], rows).astype(BF16)


def whole(shape):
    return pl.BlockSpec(shape, lambda *_: (0,) * len(shape))


def exchange(value):
    return lax.all_to_all(value, BOTH, 0, 0, tiled=True)


def spread_codebook(codebook):
    book = codebook.reshape(CENTROIDS, CHUNKS, FEATS).transpose(1, 0, 2)
    own = jnp.arange(16)[:, None] == jnp.arange(FEATS)[None, :] // SUBDIM
    spread = jnp.where(own[None, None], book[:, :, None, :], 0.0)
    spread = spread.reshape(CHUNKS, ENTRIES, FEATS)
    high = lax.reduce_precision(spread, 8, 7)
    return high.astype(BF16), (spread - high).astype(BF16)


def shards(queries, probes, targets, passage_codes, codebook):
    devices = lax.axis_size("corpus") * lax.axis_size("query")
    count = queries.shape[0]
    slots = devices * SLOTS
    list_rows = devices * CAP
    probes_t = probes.T
    big = pltpu.CompilerParams(
        dimension_semantics=("arbitrary",), vmem_limit_bytes=58 * 1024 * 1024
    )
    square = jax.ShapeDtypeStruct((devices, 128), F32)

    sending = pl.pallas_call(
        dispatch_body,
        out_shape=jax.ShapeDtypeStruct((slots, D), BF16),
        grid=(4,),
        in_specs=[whole((PROBES, count)), whole((count, D))],
        out_specs=pl.BlockSpec((slots // 4, D), lambda b: (b, 0)),
        name="dispatch",
    )(probes_t, queries)
    got = exchange(sending)
    got = pltpu.with_memory_space_constraint(got, pltpu.VMEM)
    arrived = pl.BlockSpec(memory_space=pltpu.VMEM)

    chosen, masks, notes = pl.pallas_call(
        home_body,
        out_shape=(
            jax.ShapeDtypeStruct((count, slots), BF16),
            jax.ShapeDtypeStruct((SLOTS, devices, count), BF16),
            square,
        ),
        name="home",
    )(probes_t, probes, jnp.tile(targets, (1, 128 // TARGETS)))
    high, low = spread_codebook(codebook)
    offset = (lax.axis_index("query") * OWN).astype(jnp.int32).reshape(1)

    def code_of(index):
        return pl.BlockSpec(
            (1, SUBSPACES, PASSAGES), lambda s, off: (off[0] + index(s), 0, 0)
        )

    code_specs = [
        code_of(lambda s: 0),
        code_of(lambda s: jnp.minimum(2 * s + 1, OWN - 1)),
        code_of(lambda s: jnp.minimum(2 * s + 2, OWN - 1)),
    ]
    table_spec = whole((CHUNKS, ENTRIES, FEATS))
    table = pltpu.VMEM((WIDTH // 128, slots, 128), F32)
    hot = pltpu.VMEM((WIDTH, PASSAGES), BF16)
    codes = (passage_codes,) * 3

    exps, message = pl.pallas_call(
        score_body,
        out_shape=(
            jax.ShapeDtypeStruct((OWN + 2, list_rows, PASSAGES), F32),
            jax.ShapeDtypeStruct((2 * devices, 128), F32),
        ),
        grid_spec=pltpu.PrefetchScalarGridSpec(
            num_scalar_prefetch=1,
            grid=(OWN // 2 + 1,),
            in_specs=[arrived, table_spec, table_spec, whole(square.shape)] + code_specs,
            out_specs=[
                pl.BlockSpec((2, list_rows, PASSAGES), lambda s, off: (s, 0, 0)),
                whole((2 * devices, 128)),
            ],
            scratch_shapes=[table, hot, hot]
            + [pltpu.VMEM((list_rows, PASSAGES), F32)] * 2
            + [pltpu.VMEM(square.shape, F32)],
        ),
        compiler_params=big,
        name="score",
    )(offset, got, high, low, notes, *codes)

    message = exchange(message)
    weights = pl.pallas_call(
        weight_body,
        out_shape=square,
        scratch_shapes=[pltpu.VMEM((SLOTS, devices, count), F32)],
        name="weigh",
    )(message, masks)
    teacher = pl.pallas_call(
        teacher_body,
        out_shape=jax.ShapeDtypeStruct((OWN, list_rows, PASSAGES), F32),
        grid=(OWN,),
        in_specs=[whole((2 * devices, 128))],
        out_specs=pl.BlockSpec((1, list_rows, PASSAGES), lambda i: (i, 0, 0)),
        name="teacher",
    )(message)

    def exps_of(index):
        return pl.BlockSpec((1, list_rows, PASSAGES), lambda s, off: (index(s), 0, 0))

    result = pl.pallas_call(
        grad_body,
        out_shape=jax.ShapeDtypeStruct((devices, CHUNKS * SLOTS + BOOK_ROWS, FEATS), BF16),
        grid_spec=pltpu.PrefetchScalarGridSpec(
            num_scalar_prefetch=1,
            grid=(OWN // 2,),
            in_specs=[
                whole(square.shape),
                arrived,
                table_spec,
                table_spec,
                exps_of(lambda s: 1),
                exps_of(lambda s: 2 * s + 2),
                exps_of(lambda s: jnp.minimum(2 * s + 3, OWN)),
                exps_of(lambda s: 0),
                exps_of(lambda s: 2 * s + 1),
                exps_of(lambda s: jnp.minimum(2 * s + 2, OWN - 1)),
            ]
            + code_specs,
            out_specs=whole((devices, CHUNKS * SLOTS + BOOK_ROWS, FEATS)),
            scratch_shapes=[table, hot, hot] + [pltpu.VMEM((list_rows, PASSAGES), BF16)] * 2,
        ),
        compiler_params=big,
        name="grad",
    )(
        offset, exchange(weights), got, high, low,
        exps, exps, exps, teacher, teacher, teacher, *codes,
    )

    returned = exchange(result)
    book_spec = pl.BlockSpec(
        (devices, BOOK_ROWS, FEATS), lambda b: (0, CHUNKS * SLOTS // BOOK_ROWS, 0)
    )
    book_sum = pl.pallas_call(
        book_body,
        out_shape=square,
        grid=(1,),
        in_specs=[book_spec],
        out_specs=whole(square.shape),
        name="book_sum",
    )(returned)
    normed = pl.pallas_call(
        norm_body, out_shape=jax.ShapeDtypeStruct((CENTROIDS, D), F32), name="book_norm"
    )(exchange(book_sum))
    grad_queries = pl.pallas_call(
        combine_body,
        out_shape=jax.ShapeDtypeStruct((count, D), BF16),
        grid=(1,),
        in_specs=[
            whole((count, slots)),
            pl.BlockSpec((devices, CHUNKS * SLOTS, FEATS), lambda b: (0, 0, 0)),
        ],
        out_specs=whole((count, D)),
        name="combine",
    )(chosen, returned)
    return grad_queries, normed


def solution(mesh):
    placed = (
        P(BOTH, None),
        P(BOTH, None),
        P(BOTH, None),
        P("corpus", None, None),
        P(),
    )

    return jax.shard_map(
        shards,
        mesh=mesh,
        in_specs=placed,
        out_specs=(P(BOTH, None), P()),
        check_vma=False,
    )
```

```python
import jax
import jax.numpy as jnp
from jax import lax
from jax.experimental import pallas as pl
from jax.experimental.pallas import tpu as pltpu
from jax.sharding import PartitionSpec as P


D = 768
SUBSPACES = 96
CENTROIDS = 16
SUBDIM = 8
PASSAGES = 1024
PROBES = 4
TARGETS = 8
CAP = 2
EPSILON = 1e-06

BOTH = ("corpus", "query")
CHUNKS = 6
FEATS = 128
ENTRIES = 256
WIDTH = SUBSPACES * CENTROIDS
OWN = 8
SLOTS = OWN * CAP
BOOK_ROWS = 8
F32 = jnp.float32
BF16 = jnp.bfloat16


def dot(a, b, dims=((1,), (0,))):
    return lax.dot_general(a, b, (dims, ((), ())), preferred_element_type=F32)


def iota(shape, axis):
    return lax.broadcasted_iota(jnp.int32, shape, axis)


def ones_where(mask):
    return jnp.where(mask, 1.0, 0.0).astype(BF16)


def split_two(value):
    high = value.astype(BF16)
    return high, (value - high.astype(F32)).astype(BF16)


def names_list(probe_rows, lists):
    found = probe_rows[0:1, :] == lists
    for p in range(1, PROBES):
        found = found | (probe_rows[p : p + 1, :] == lists)
    return found


def dispatch_body(probes_t, queries, sending):
    count = queries.shape[0]
    rows = sending.shape[0] // CAP
    lists = iota((rows, count), 0) + pl.program_id(0) * rows
    found = names_list(probes_t[...], lists)
    before = ones_where(iota((count, count), 0) < iota((count, count), 1))
    rank = dot(ones_where(found), before)
    chosen = [
        jnp.where(found & (rank == float(r)), 1.0, 0.0).reshape(rows // OWN, 1, OWN, count)
        for r in range(CAP)
    ]
    chosen = jnp.concatenate(chosen, axis=1).reshape(rows * CAP, count).astype(BF16)
    sending[...] = dot(chosen, queries[...]).astype(BF16)


def home_body(probes_t, probes, targets_wide, chosen_out, masks_out, notes_out):
    count = probes.shape[0]
    slots = chosen_out.shape[1]
    devices = notes_out.shape[0]
    block = 512
    after = ones_where(iota((count, count), 0) > iota((count, count), 1))
    for b in range(slots // block):
        slot = iota((count, block), 1) + b * block
        lists = (slot // SLOTS) * OWN + (slot & (OWN - 1))
        found = probes[:, 0:1] == lists
        for p in range(1, PROBES):
            found = found | (probes[:, p : p + 1] == lists)
        rank = dot(after, ones_where(found))
        wanted = ((slot // OWN) & 1).astype(F32)
        chosen_out[:, b * block : (b + 1) * block] = ones_where(found & (rank == wanted))
    wide = targets_wide[...]
    spot = wide & (PASSAGES - 1)
    column = wide // PASSAGES
    in_list = jnp.broadcast_to(probes[:, 0:1], wide.shape)
    for p in range(1, PROBES):
        in_list = jnp.where(column == p, probes[:, p : p + 1], in_list)
    parts = jnp.concatenate(
        [in_list >> 5, in_list & 31, spot >> 5, spot & 31], axis=1
    ).astype(F32).astype(BF16)
    before = ones_where(iota((count, count), 0) < iota((count, count), 1))
    lane = iota((devices, 128), 1)
    gathered = jnp.zeros((devices, 4 * 128), F32)
    lane_wide = iota((devices, 4 * 128), 1) & 127
    for i in range(OWN):
        found = names_list(probes_t[...], iota((devices, count), 0) * OWN + i)
        rank = dot(ones_where(found), before)
        for r in range(CAP):
            mask = ones_where(found & (rank == float(r)))
            masks_out[r * OWN + i] = mask
            here = dot(mask, parts)
            gathered = jnp.where(lane_wide // TARGETS == r * OWN + i, here, gathered)
    got_list = gathered[:, 0:128] * 32.0 + gathered[:, 128:256]
    got_spot = gathered[:, 256:384] * 32.0 + gathered[:, 384:512]
    own_list = iota((devices, 128), 0) * OWN + ((lane // TARGETS) & (OWN - 1))
    notes_out[...] = jnp.where(got_list == own_list.astype(F32), got_spot + 1.0, 0.0)


def fill_one_hot(codes, one_hot):
    for c in range(CHUNKS):
        part = codes[0, c * 16 : (c + 1) * 16, :].astype(F32).astype(BF16)
        for k in range(CENTROIDS):
            at = c * ENTRIES + k * 16
            one_hot[at : at + 16, :] = jnp.where(
                part == jnp.asarray(k, BF16), jnp.asarray(1, BF16), jnp.asarray(0, BF16)
            )


def score_body(
    offset, got_far, high, low, notes, odd, even,
    exps, message, table, hot_a, hot_b, held_a, held_b, stats, got, sems,
):
    s = pl.program_id(0)
    half = stats.shape[0]

    def score(i, hot, held):
        rows = jnp.concatenate(
            [
                jnp.concatenate(
                    [
                        table[j, pl.ds(r * OWN + i, half, stride=SLOTS), :].astype(BF16)
                        for j in range(WIDTH // 128)
                    ],
                    axis=1,
                )
                for r in range(CAP)
            ],
            axis=0,
        )
        held[...] = dot(rows, hot[...])

    def soften(i, held, place):
        scores = held[...]
        top = jnp.max(scores, axis=1, keepdims=True)
        exp_scores = jnp.exp(scores - top)
        total = jnp.sum(exp_scores, axis=1, keepdims=True)
        exps[place] = exp_scores
        lane = iota(stats.shape, 1)
        kept = stats[...]
        for r in range(CAP):
            at = r * OWN + i
            kept = jnp.where(lane == at, top[r * half : (r + 1) * half], kept)
            kept = jnp.where(lane == SLOTS + at, total[r * half : (r + 1) * half], kept)
        stats[...] = kept

    last = pl.num_programs(0) - 1

    @pl.when(s == 0)
    def _():
        copies = [
            pltpu.make_async_copy(
                got_far.at[:, c * FEATS : (c + 1) * FEATS], got.at[c], sems.at[c]
            )
            for c in range(CHUNKS)
        ]
        for copy in copies:
            copy.start()
        stats[...] = jnp.zeros_like(stats)
        held_b[...] = jnp.zeros_like(held_b)
        fill_one_hot(even, hot_a)
        for c in range(CHUNKS):
            copies[c].wait()
            twice = jnp.concatenate([got[c], got[c]], axis=1)
            weights = jnp.concatenate([high[c], low[c]], axis=1)
            looked = dot(twice, weights, ((1,), (1,)))
            table[2 * c] = looked[:, 0:128]
            table[2 * c + 1] = looked[:, 128:256]

    @pl.when((s > 0) & (s < last))
    def _():
        score(2 * s - 2, hot_a, held_a)
        fill_one_hot(odd, hot_b)
        soften(2 * s - 3, held_b, 0)
        score(2 * s - 1, hot_b, held_b)
        fill_one_hot(even, hot_a)
        soften(2 * s - 2, held_a, 1)

    @pl.when(s == last)
    def _():
        soften(2 * s - 3, held_b, 0)
        exps[1] = jnp.zeros(exps.shape[1:], F32)
        message[...] = jnp.stack([stats[...], notes[...]], axis=1).reshape(message.shape)


def weight_body(stats, masks, weights, ratios):
    devices, count = masks.shape[1:]
    tops = stats[pl.ds(0, devices, stride=2), :]
    low = -3.0e38
    peak = jnp.full((devices, count), low, F32)
    for s in range(SLOTS):
        peak = jnp.maximum(peak, jnp.where(masks[s] > 0, tops[:, s : s + 1], low))
    peak = jnp.max(peak, axis=0, keepdims=True)
    denom = jnp.zeros((devices, count), F32)
    for s in range(SLOTS):
        ratio = jnp.where(masks[s] > 0, jnp.exp(tops[:, s : s + 1] - peak), 0.0)
        ratios[s] = ratio
        denom = denom + ratio * tops[:, SLOTS + s : SLOTS + 1 + s]
    denom = jnp.sum(denom, axis=0, keepdims=True)
    lane = iota((devices, 128), 1)
    held = jnp.zeros((devices, 128), F32)
    for s in range(SLOTS):
        part = jnp.sum(ratios[s] / denom, axis=1, keepdims=True)
        held = jnp.where(lane == s, part, held)
    weights[...] = held


def teacher_body(message, teacher):
    i = pl.program_id(0)
    half = message.shape[0] // 2
    turned = pltpu.roll(message[pl.ds(1, half, stride=2), :], (128 - TARGETS * i) % 128, 1)
    place = iota((half, PASSAGES), 1).astype(F32)
    for r in range(CAP):
        held = jnp.zeros((half, PASSAGES), F32)
        for t in range(TARGETS):
            at = r * OWN * TARGETS + t
            weight = 2.0 * (TARGETS - t) / (TARGETS * (TARGETS + 1.0))
            held = jnp.where(place == turned[:, at : at + 1] - 1.0, weight, held)
        teacher[0, r * half : (r + 1) * half, :] = held


def grad_body(
    offset, weights, got_far, high, low, exps_odd, exps_even, teacher_odd, teacher_even,
    odd, even, out, hist, hot_a, hot_b, grads_a, grads_b, got, sems,
):
    s = pl.program_id(0)
    half = weights.shape[0]

    def prepare(i, exps, teacher, codes, hot, grads):
        lane = iota((half, 128), 1)
        for r in range(CAP):
            own = jnp.where(lane == r * OWN + i, weights[...], 0.0)
            scale = jnp.sum(own, axis=1, keepdims=True)
            rows = slice(r * half, (r + 1) * half)
            grads[rows, :] = (exps[0, rows, :] * scale - teacher[0, rows, :]).astype(BF16)
        fill_one_hot(codes, hot)

    def count(i, hot, grads):
        found = dot(grads[...], hot[...], ((1,), (1,)))
        for r in range(CAP):
            for j in range(WIDTH // 128):
                hist[j, pl.ds(r * OWN + i, half, stride=SLOTS), :] = found[
                    r * half : (r + 1) * half, j * 128 : (j + 1) * 128
                ]

    copies = [
        pltpu.make_async_copy(got_far.at[:, c * FEATS : (c + 1) * FEATS], got.at[c], sems.at[c])
        for c in range(CHUNKS)
    ]
    following = jnp.minimum(2 * s, OWN - 1)

    @pl.when(s == 0)
    def _():
        prepare(0, exps_even, teacher_even, even, hot_a, grads_a)
        for copy in copies:
            copy.start()

    @pl.when(s > 0)
    def _():
        count(2 * s - 2, hot_a, grads_a)
        prepare(2 * s - 1, exps_odd, teacher_odd, odd, hot_b, grads_b)
        count(2 * s - 1, hot_b, grads_b)
        prepare(following, exps_even, teacher_even, even, hot_a, grads_a)

    @pl.when(s == pl.num_programs(0) - 1)
    def _():
        for copy in copies:
            copy.wait()
        devices = out.shape[0]
        keep = iota((ENTRIES, FEATS), 0) % 16 == iota((ENTRIES, FEATS), 1) // SUBDIM
        top = CHUNKS * SLOTS
        out[CHUNKS * CENTROIDS :, top:, :] = jnp.zeros(
            (devices - CHUNKS * CENTROIDS, BOOK_ROWS, 128), BF16
        )
        for c in range(CHUNKS):
            h_high, h_low = split_two(jnp.concatenate([hist[2 * c], hist[2 * c + 1]], axis=1))
            both = jnp.concatenate([high[c], low[c]], axis=1)
            wide = dot(h_high, both)
            part = wide[:, 0:FEATS] + wide[:, FEATS:] + dot(h_low, high[c])
            out[:, c * SLOTS : (c + 1) * SLOTS, :] = part.reshape(devices, SLOTS, FEATS).astype(
                BF16
            )
            book = dot(got[c], h_high, ((0,), (0,)))
            book = jnp.where(keep, book.T, 0.0)
            book = jnp.sum(book.reshape(CENTROIDS, 16, FEATS), axis=1)
            b_high = book.astype(BF16)
            b_rest = book - b_high.astype(F32)
            b_mid = b_rest.astype(BF16)
            b_low = b_rest - b_mid.astype(F32)
            row = iota((CENTROIDS, BOOK_ROWS, FEATS), 1)
            parts = jnp.where(row == 0, b_high.astype(F32)[:, None, :], 0.0)
            parts = jnp.where(row == 1, b_mid.astype(F32)[:, None, :], parts)
            parts = jnp.where(row == 2, b_low[:, None, :], parts)
            out[c * CENTROIDS : (c + 1) * CENTROIDS, top:, :] = parts.astype(BF16)


def book_body(returned, total):
    parts = returned[...].astype(F32)
    total[...] = jnp.broadcast_to(
        jnp.sum(jnp.sum(parts, axis=0), axis=0, keepdims=True), total.shape
    )


def norm_body(rows, normed):
    value = rows[0 : CHUNKS * CENTROIDS, :]
    mean = jnp.sum(value * value, keepdims=True) / (CENTROIDS * D)
    value = value * lax.rsqrt(mean + EPSILON)
    for c in range(CHUNKS):
        normed[:, c * FEATS : (c + 1) * FEATS] = value[c * CENTROIDS : (c + 1) * CENTROIDS]


def combine_body(chosen, returned, out):
    devices = returned.shape[0]
    for c in range(CHUNKS):
        rows = returned[:, c * SLOTS : (c + 1) * SLOTS, :].reshape(devices * SLOTS, FEATS)
        out[:, c * FEATS : (c + 1) * FEATS] = dot(chosen[...], rows).astype(BF16)


def whole(shape):
    return pl.BlockSpec(shape, lambda *_: (0,) * len(shape))


def exchange(value):
    return lax.all_to_all(value, BOTH, 0, 0, tiled=True)


def uncopied(value):
    return pltpu.with_memory_space_constraint(value, pltpu.VMEM)


def spread_codebook(codebook):
    book = codebook.reshape(CENTROIDS, CHUNKS, FEATS).transpose(1, 0, 2)
    own = jnp.arange(16)[:, None] == jnp.arange(FEATS)[None, :] // SUBDIM
    spread = jnp.where(own[None, None], book[:, :, None, :], 0.0)
    spread = spread.reshape(CHUNKS, ENTRIES, FEATS)
    high = lax.reduce_precision(spread, 8, 7)
    return high.astype(BF16), (spread - high).astype(BF16)


def shards(queries, probes, targets, passage_codes, codebook):
    devices = lax.axis_size("corpus") * lax.axis_size("query")
    count = queries.shape[0]
    slots = devices * SLOTS
    list_rows = devices * CAP
    probes_t = probes.T
    big = pltpu.CompilerParams(
        dimension_semantics=("arbitrary",), vmem_limit_bytes=58 * 1024 * 1024
    )
    square = jax.ShapeDtypeStruct((devices, 128), F32)

    sending = pl.pallas_call(
        dispatch_body,
        out_shape=jax.ShapeDtypeStruct((slots, D), BF16),
        grid=(4,),
        in_specs=[whole((PROBES, count)), whole((count, D))],
        out_specs=pl.BlockSpec((slots // 4, D), lambda b: (b, 0)),
        name="dispatch",
    )(probes_t, queries)
    got = uncopied(exchange(sending))
    arrived = pl.BlockSpec(memory_space=pl.ANY)
    arrived_here = pltpu.VMEM((CHUNKS, slots, FEATS), BF16)

    chosen, masks, notes = pl.pallas_call(
        home_body,
        out_shape=(
            jax.ShapeDtypeStruct((count, slots), BF16),
            jax.ShapeDtypeStruct((SLOTS, devices, count), BF16),
            square,
        ),
        name="home",
    )(probes_t, probes, jnp.tile(targets, (1, 128 // TARGETS)))
    high, low = spread_codebook(codebook)
    offset = (lax.axis_index("query") * OWN).astype(jnp.int32).reshape(1)

    def code_of(index):
        return pl.BlockSpec(
            (1, SUBSPACES, PASSAGES), lambda s, off: (off[0] + index(s), 0, 0)
        )

    def in_order(index_of):
        return [
            index_of(lambda s: jnp.clip(2 * s - 1, 1, OWN - 1)),
            index_of(lambda s: jnp.minimum(2 * s, OWN - 1)),
        ]

    code_specs = in_order(code_of)
    table_spec = whole((CHUNKS, ENTRIES, FEATS))
    table = pltpu.VMEM((WIDTH // 128, slots, 128), F32)
    hot = pltpu.VMEM((WIDTH, PASSAGES), BF16)
    codes = (passage_codes,) * 2

    exps, message = pl.pallas_call(
        score_body,
        out_shape=(
            jax.ShapeDtypeStruct((OWN + 2, list_rows, PASSAGES), F32),
            jax.ShapeDtypeStruct((2 * devices, 128), F32),
        ),
        grid_spec=pltpu.PrefetchScalarGridSpec(
            num_scalar_prefetch=1,
            grid=(OWN // 2 + 2,),
            in_specs=[arrived, table_spec, table_spec, whole(square.shape)] + code_specs,
            out_specs=[
                pl.BlockSpec(
                    (2, list_rows, PASSAGES), lambda s, off: (jnp.maximum(s - 1, 0), 0, 0)
                ),
                whole((2 * devices, 128)),
            ],
            scratch_shapes=[table, hot, hot]
            + [pltpu.VMEM((list_rows, PASSAGES), F32)] * 2
            + [pltpu.VMEM(square.shape, F32), arrived_here, pltpu.SemaphoreType.DMA((CHUNKS,))],
        ),
        compiler_params=big,
        name="score",
    )(offset, got, high, low, notes, *codes)

    message = exchange(message)
    weights = pl.pallas_call(
        weight_body,
        out_shape=square,
        scratch_shapes=[pltpu.VMEM((SLOTS, devices, count), F32)],
        name="weigh",
    )(message, masks)
    teacher = pl.pallas_call(
        teacher_body,
        out_shape=jax.ShapeDtypeStruct((OWN, list_rows, PASSAGES), F32),
        grid=(OWN,),
        in_specs=[whole((2 * devices, 128))],
        out_specs=pl.BlockSpec((1, list_rows, PASSAGES), lambda i: (i, 0, 0)),
        name="teacher",
    )(message)

    def exps_of(index):
        return pl.BlockSpec((1, list_rows, PASSAGES), lambda s, off: (index(s), 0, 0))

    result = pl.pallas_call(
        grad_body,
        out_shape=jax.ShapeDtypeStruct((devices, CHUNKS * SLOTS + BOOK_ROWS, FEATS), BF16),
        grid_spec=pltpu.PrefetchScalarGridSpec(
            num_scalar_prefetch=1,
            grid=(OWN // 2 + 1,),
            in_specs=[
                whole(square.shape),
                arrived,
                table_spec,
                table_spec,
            ]
            + in_order(lambda index: exps_of(lambda s: index(s) + 1))
            + in_order(exps_of)
            + code_specs,
            out_specs=whole((devices, CHUNKS * SLOTS + BOOK_ROWS, FEATS)),
            scratch_shapes=[table, hot, hot]
            + [pltpu.VMEM((list_rows, PASSAGES), BF16)] * 2
            + [arrived_here, pltpu.SemaphoreType.DMA((CHUNKS,))],
        ),
        compiler_params=big,
        name="grad",
    )(
        offset, uncopied(exchange(weights)), got, high, low,
        exps, exps, teacher, teacher, *codes,
    )

    returned = exchange(result)
    book_spec = pl.BlockSpec(
        (devices, BOOK_ROWS, FEATS), lambda b: (0, CHUNKS * SLOTS // BOOK_ROWS, 0)
    )
    book_sum = pl.pallas_call(
        book_body,
        out_shape=square,
        grid=(1,),
        in_specs=[book_spec],
        out_specs=whole(square.shape),
        name="book_sum",
    )(returned)
    normed = pl.pallas_call(
        norm_body, out_shape=jax.ShapeDtypeStruct((CENTROIDS, D), F32), name="book_norm"
    )(uncopied(exchange(book_sum)))
    grad_queries = pl.pallas_call(
        combine_body,
        out_shape=jax.ShapeDtypeStruct((count, D), BF16),
        grid=(1,),
        in_specs=[
            whole((count, slots)),
            pl.BlockSpec((devices, CHUNKS * SLOTS, FEATS), lambda b: (0, 0, 0)),
        ],
        out_specs=whole((count, D)),
        name="combine",
    )(chosen, returned)
    return grad_queries, normed


def solution(mesh):
    placed = (
        P(BOTH, None),
        P(BOTH, None),
        P(BOTH, None),
        P("corpus", None, None),
        P(),
    )

    return jax.shard_map(
        shards,
        mesh=mesh,
        in_specs=placed,
        out_specs=(P(BOTH, None), P()),
        check_vma=False,
    )
```

```python
import jax
import jax.numpy as jnp
from jax import lax
from jax.experimental import pallas as pl
from jax.experimental.pallas import tpu as pltpu
from jax.sharding import PartitionSpec as P


D = 768
SUBSPACES = 96
CENTROIDS = 16
SUBDIM = 8
PASSAGES = 1024
PROBES = 4
TARGETS = 8
CAP = 2
EPSILON = 1e-06

BOTH = ("corpus", "query")
CHUNKS = 6
FEATS = 128
ENTRIES = 256
WIDTH = SUBSPACES * CENTROIDS
OWN = 8
SLOTS = OWN * CAP
BOOK_ROWS = 8
F32 = jnp.float32
BF16 = jnp.bfloat16


def dot(a, b, dims=((1,), (0,))):
    return lax.dot_general(a, b, (dims, ((), ())), preferred_element_type=F32)


def iota(shape, axis):
    return lax.broadcasted_iota(jnp.int32, shape, axis)


def ones_where(mask):
    return jnp.where(mask, 1.0, 0.0).astype(BF16)


def split_two(value):
    high = value.astype(BF16)
    return high, (value - high.astype(F32)).astype(BF16)


def names_list(probe_rows, lists):
    found = probe_rows[0:1, :] == lists
    for p in range(1, PROBES):
        found = found | (probe_rows[p : p + 1, :] == lists)
    return found


def dispatch_body(probes_t, queries, sending):
    count = queries.shape[0]
    rows = sending.shape[0] // CAP
    lists = iota((rows, count), 0) + pl.program_id(0) * rows
    found = names_list(probes_t[...], lists)
    before = ones_where(iota((count, count), 0) < iota((count, count), 1))
    rank = dot(ones_where(found), before)
    chosen = [
        jnp.where(found & (rank == float(r)), 1.0, 0.0).reshape(rows // OWN, 1, OWN, count)
        for r in range(CAP)
    ]
    chosen = jnp.concatenate(chosen, axis=1).reshape(rows * CAP, count).astype(BF16)
    sending[...] = dot(chosen, queries[...]).astype(BF16)


def home_body(probes_t, probes, targets_wide, chosen_out, masks_out, notes_out):
    count = probes.shape[0]
    slots = chosen_out.shape[1]
    devices = notes_out.shape[0]
    block = 512
    after = ones_where(iota((count, count), 0) > iota((count, count), 1))
    for b in range(slots // block):
        slot = iota((count, block), 1) + b * block
        lists = (slot // SLOTS) * OWN + (slot & (OWN - 1))
        found = probes[:, 0:1] == lists
        for p in range(1, PROBES):
            found = found | (probes[:, p : p + 1] == lists)
        rank = dot(after, ones_where(found))
        wanted = ((slot // OWN) & 1).astype(F32)
        chosen_out[:, b * block : (b + 1) * block] = ones_where(found & (rank == wanted))
    wide = targets_wide[...]
    spot = wide & (PASSAGES - 1)
    column = wide // PASSAGES
    in_list = jnp.broadcast_to(probes[:, 0:1], wide.shape)
    for p in range(1, PROBES):
        in_list = jnp.where(column == p, probes[:, p : p + 1], in_list)
    parts = jnp.concatenate(
        [in_list >> 5, in_list & 31, spot >> 5, spot & 31], axis=1
    ).astype(F32).astype(BF16)
    before = ones_where(iota((count, count), 0) < iota((count, count), 1))
    lane = iota((devices, 128), 1)
    gathered = jnp.zeros((devices, 4 * 128), F32)
    lane_wide = iota((devices, 4 * 128), 1) & 127
    for i in range(OWN):
        found = names_list(probes_t[...], iota((devices, count), 0) * OWN + i)
        rank = dot(ones_where(found), before)
        for r in range(CAP):
            mask = ones_where(found & (rank == float(r)))
            masks_out[r * OWN + i] = mask
            here = dot(mask, parts)
            gathered = jnp.where(lane_wide // TARGETS == r * OWN + i, here, gathered)
    got_list = gathered[:, 0:128] * 32.0 + gathered[:, 128:256]
    got_spot = gathered[:, 256:384] * 32.0 + gathered[:, 384:512]
    own_list = iota((devices, 128), 0) * OWN + ((lane // TARGETS) & (OWN - 1))
    notes_out[...] = jnp.where(got_list == own_list.astype(F32), got_spot + 1.0, 0.0)


def fill_one_hot(codes, one_hot):
    for c in range(CHUNKS):
        part = codes[0, c * 16 : (c + 1) * 16, :].astype(F32).astype(BF16)
        for k in range(CENTROIDS):
            at = c * ENTRIES + k * 16
            one_hot[at : at + 16, :] = jnp.where(
                part == jnp.asarray(k, BF16), jnp.asarray(1, BF16), jnp.asarray(0, BF16)
            )


def score_body(
    offset, got_far, high, low, notes, odd, even,
    exps, message, table, hot_a, hot_b, held_a, held_b, stats, got, second, sem,
):
    s = pl.program_id(0)
    half = stats.shape[0]

    def score(i, hot, held, ranks):
        rows = [
            jnp.concatenate(
                [
                    table[j, pl.ds(r * OWN + i, half, stride=SLOTS), :].astype(BF16)
                    for j in range(WIDTH // 128)
                ],
                axis=1,
            )
            for r in range(ranks)
        ]
        held[0 : ranks * half, :] = dot(jnp.concatenate(rows, axis=0), hot[...])
        if ranks < CAP:
            held[ranks * half :, :] = jnp.zeros((held.shape[0] - ranks * half, PASSAGES), F32)

    def soften(i, held, place):
        scores = held[...]
        top = jnp.max(scores, axis=1, keepdims=True)
        exp_scores = jnp.exp(scores - top)
        total = jnp.sum(exp_scores, axis=1, keepdims=True)
        exps[place] = exp_scores
        lane = iota(stats.shape, 1)
        kept = stats[...]
        for r in range(CAP):
            at = r * OWN + i
            kept = jnp.where(lane == at, top[r * half : (r + 1) * half], kept)
            kept = jnp.where(lane == SLOTS + at, total[r * half : (r + 1) * half], kept)
        stats[...] = kept

    last = pl.num_programs(0) - 1

    @pl.when(s == 0)
    def _():
        copy = pltpu.make_async_copy(got_far, got, sem)
        copy.start()
        stats[...] = jnp.zeros_like(stats)
        held_b[...] = jnp.zeros_like(held_b)
        fill_one_hot(even, hot_a)
        copy.wait()
        for c in range(CHUNKS):
            rows = got[:, c * FEATS : (c + 1) * FEATS]
            twice = jnp.concatenate([rows, rows], axis=1)
            weights = jnp.concatenate([high[c], low[c]], axis=1)
            looked = dot(twice, weights, ((1,), (1,)))
            table[2 * c] = looked[:, 0:128]
            table[2 * c + 1] = looked[:, 128:256]
        size = jnp.zeros((SLOTS, FEATS), F32)
        for c in range(CHUNKS):
            rows = jnp.abs(got[:, c * FEATS : (c + 1) * FEATS])
            while rows.shape[0] > SLOTS:
                middle = rows.shape[0] // 2
                rows = jnp.maximum(rows[:middle], rows[middle:])
            size = jnp.maximum(size, rows.astype(F32))
        slot = iota(size.shape, 0)
        for pair in range(OWN // 2):
            at = OWN + 2 * pair
            second[pair] = jnp.max(jnp.where((slot == at) | (slot == at + 1), size, 0.0))

    def step(ranks):
        score(2 * s - 2, hot_a, held_a, ranks)
        fill_one_hot(odd, hot_b)
        soften(2 * s - 3, held_b, 0)
        score(2 * s - 1, hot_b, held_b, ranks)
        fill_one_hot(even, hot_a)
        soften(2 * s - 2, held_a, 1)

    inside = (s > 0) & (s < last)
    filled = second[jnp.clip(s - 1, 0, OWN // 2 - 1)] > 0.0

    @pl.when(inside & filled)
    def _():
        step(CAP)

    @pl.when(inside & jnp.logical_not(filled))
    def _():
        step(1)

    @pl.when(s == last)
    def _():
        soften(2 * s - 3, held_b, 0)
        exps[1] = jnp.zeros(exps.shape[1:], F32)
        message[...] = jnp.stack([stats[...], notes[...]], axis=1).reshape(message.shape)


def weight_body(stats, masks, weights, ratios):
    devices, count = masks.shape[1:]
    tops = stats[pl.ds(0, devices, stride=2), :]
    low = -3.0e38
    peak = jnp.full((devices, count), low, F32)
    for s in range(SLOTS):
        peak = jnp.maximum(peak, jnp.where(masks[s] > 0, tops[:, s : s + 1], low))
    peak = jnp.max(peak, axis=0, keepdims=True)
    denom = jnp.zeros((devices, count), F32)
    for s in range(SLOTS):
        ratio = jnp.where(masks[s] > 0, jnp.exp(tops[:, s : s + 1] - peak), 0.0)
        ratios[s] = ratio
        denom = denom + ratio * tops[:, SLOTS + s : SLOTS + 1 + s]
    denom = jnp.sum(denom, axis=0, keepdims=True)
    lane = iota((devices, 128), 1)
    held = jnp.zeros((devices, 128), F32)
    for s in range(SLOTS):
        part = jnp.sum(ratios[s] / denom, axis=1, keepdims=True)
        held = jnp.where(lane == s, part, held)
    weights[...] = held


def teacher_body(message, teacher):
    i = pl.program_id(0)
    half = message.shape[0] // 2
    turned = pltpu.roll(message[pl.ds(1, half, stride=2), :], (128 - TARGETS * i) % 128, 1)
    place = iota((half, PASSAGES), 1).astype(F32)
    for r in range(CAP):
        held = jnp.zeros((half, PASSAGES), F32)
        for t in range(TARGETS):
            at = r * OWN * TARGETS + t
            weight = 2.0 * (TARGETS - t) / (TARGETS * (TARGETS + 1.0))
            held = jnp.where(place == turned[:, at : at + 1] - 1.0, weight, held)
        teacher[0, r * half : (r + 1) * half, :] = held


def grad_body(
    offset, weights, message, got_far, high, low, exps_odd, exps_even, teacher_odd, teacher_even,
    odd, even, out, hist, hot_a, hot_b, grads_a, grads_b, got, second, sems,
):
    s = pl.program_id(0)
    half = weights.shape[0]

    def prepare(i, exps, teacher, codes, hot, grads):
        lane = iota((half, 128), 1)
        for r in range(CAP):
            own = jnp.where(lane == r * OWN + i, weights[...], 0.0)
            scale = jnp.sum(own, axis=1, keepdims=True)
            rows = slice(r * half, (r + 1) * half)
            grads[rows, :] = (exps[0, rows, :] * scale - teacher[0, rows, :]).astype(BF16)
        fill_one_hot(codes, hot)

    def count(i, hot, grads, ranks):
        found = dot(grads[0 : ranks * half, :], hot[...], ((1,), (1,)))
        for r in range(ranks):
            for j in range(WIDTH // 128):
                hist[j, pl.ds(r * OWN + i, half, stride=SLOTS), :] = found[
                    r * half : (r + 1) * half, j * 128 : (j + 1) * 128
                ]

    copies = [
        pltpu.make_async_copy(got_far.at[:, c * FEATS : (c + 1) * FEATS], got.at[c], sems.at[c])
        for c in range(CHUNKS)
    ]
    following = jnp.minimum(2 * s, OWN - 1)

    @pl.when(s == 0)
    def _():
        prepare(0, exps_even, teacher_even, even, hot_a, grads_a)
        for copy in copies:
            copy.start()
        for row in range(half):
            at = row * SLOTS + OWN
            hist[:, at : at + OWN, :] = jnp.zeros((hist.shape[0], OWN, 128), F32)
        weight = jnp.max(jnp.abs(weights[...]), axis=0, keepdims=True)
        note = jnp.max(message[pl.ds(1, half, stride=2), :], axis=0, keepdims=True)
        lane = iota(weight.shape, 1)
        for pair in range(OWN // 2):
            at = OWN + 2 * pair
            held = jnp.where((lane == at) | (lane == at + 1), weight, 0.0)
            noted = jnp.where(lane // (2 * TARGETS) == at // 2, note, 0.0)
            second[pair] = jnp.maximum(jnp.max(held), jnp.max(noted))

    def step(ranks):
        count(2 * s - 2, hot_a, grads_a, ranks)
        prepare(2 * s - 1, exps_odd, teacher_odd, odd, hot_b, grads_b)
        count(2 * s - 1, hot_b, grads_b, ranks)
        prepare(following, exps_even, teacher_even, even, hot_a, grads_a)

    filled = second[jnp.maximum(s - 1, 0)] > 0.0

    @pl.when((s > 0) & filled)
    def _():
        step(CAP)

    @pl.when((s > 0) & jnp.logical_not(filled))
    def _():
        step(1)

    @pl.when(s == pl.num_programs(0) - 1)
    def _():
        for copy in copies:
            copy.wait()
        devices = out.shape[0]
        keep = iota((ENTRIES, FEATS), 0) % 16 == iota((ENTRIES, FEATS), 1) // SUBDIM
        top = CHUNKS * SLOTS
        out[CHUNKS * CENTROIDS :, top:, :] = jnp.zeros(
            (devices - CHUNKS * CENTROIDS, BOOK_ROWS, 128), BF16
        )
        for c in range(CHUNKS):
            h_high, h_low = split_two(jnp.concatenate([hist[2 * c], hist[2 * c + 1]], axis=1))
            both = jnp.concatenate([high[c], low[c]], axis=1)
            wide = dot(h_high, both)
            part = wide[:, 0:FEATS] + wide[:, FEATS:] + dot(h_low, high[c])
            out[:, c * SLOTS : (c + 1) * SLOTS, :] = part.reshape(devices, SLOTS, FEATS).astype(
                BF16
            )
            book = dot(got[c], h_high, ((0,), (0,)))
            book = jnp.where(keep, book.T, 0.0)
            book = jnp.sum(book.reshape(CENTROIDS, 16, FEATS), axis=1)
            b_high = book.astype(BF16)
            b_rest = book - b_high.astype(F32)
            b_mid = b_rest.astype(BF16)
            b_low = b_rest - b_mid.astype(F32)
            row = iota((CENTROIDS, BOOK_ROWS, FEATS), 1)
            parts = jnp.where(row == 0, b_high.astype(F32)[:, None, :], 0.0)
            parts = jnp.where(row == 1, b_mid.astype(F32)[:, None, :], parts)
            parts = jnp.where(row == 2, b_low[:, None, :], parts)
            out[c * CENTROIDS : (c + 1) * CENTROIDS, top:, :] = parts.astype(BF16)


def book_body(returned, total):
    parts = returned[...].astype(F32)
    total[...] = jnp.broadcast_to(
        jnp.sum(jnp.sum(parts, axis=0), axis=0, keepdims=True), total.shape
    )


def norm_body(rows, normed):
    value = rows[0 : CHUNKS * CENTROIDS, :]
    mean = jnp.sum(value * value, keepdims=True) / (CENTROIDS * D)
    value = value * lax.rsqrt(mean + EPSILON)
    for c in range(CHUNKS):
        normed[:, c * FEATS : (c + 1) * FEATS] = value[c * CENTROIDS : (c + 1) * CENTROIDS]


def combine_body(chosen, returned, out):
    devices = returned.shape[0]
    for c in range(CHUNKS):
        rows = returned[:, c * SLOTS : (c + 1) * SLOTS, :].reshape(devices * SLOTS, FEATS)
        out[:, c * FEATS : (c + 1) * FEATS] = dot(chosen[...], rows).astype(BF16)


def whole(shape):
    return pl.BlockSpec(shape, lambda *_: (0,) * len(shape))


def exchange(value):
    return lax.all_to_all(value, BOTH, 0, 0, tiled=True)


def uncopied(value):
    return pltpu.with_memory_space_constraint(value, pltpu.VMEM)


def spread_codebook(codebook):
    book = codebook.reshape(CENTROIDS, CHUNKS, FEATS).transpose(1, 0, 2)
    own = jnp.arange(16)[:, None] == jnp.arange(FEATS)[None, :] // SUBDIM
    spread = jnp.where(own[None, None], book[:, :, None, :], 0.0)
    spread = spread.reshape(CHUNKS, ENTRIES, FEATS)
    high = lax.reduce_precision(spread, 8, 7)
    return high.astype(BF16), (spread - high).astype(BF16)


def shards(queries, probes, targets, passage_codes, codebook):
    devices = lax.axis_size("corpus") * lax.axis_size("query")
    count = queries.shape[0]
    slots = devices * SLOTS
    list_rows = devices * CAP
    probes_t = probes.T
    big = pltpu.CompilerParams(
        dimension_semantics=("arbitrary",), vmem_limit_bytes=58 * 1024 * 1024
    )
    square = jax.ShapeDtypeStruct((devices, 128), F32)

    sending = pl.pallas_call(
        dispatch_body,
        out_shape=jax.ShapeDtypeStruct((slots, D), BF16),
        grid=(4,),
        in_specs=[whole((PROBES, count)), whole((count, D))],
        out_specs=pl.BlockSpec((slots // 4, D), lambda b: (b, 0)),
        name="dispatch",
    )(probes_t, queries)
    got = uncopied(exchange(sending))
    arrived = pl.BlockSpec(memory_space=pl.ANY)
    arrived_here = pltpu.VMEM((CHUNKS, slots, FEATS), BF16)

    chosen, masks, notes = pl.pallas_call(
        home_body,
        out_shape=(
            jax.ShapeDtypeStruct((count, slots), BF16),
            jax.ShapeDtypeStruct((SLOTS, devices, count), BF16),
            square,
        ),
        name="home",
    )(probes_t, probes, jnp.tile(targets, (1, 128 // TARGETS)))
    high, low = spread_codebook(codebook)
    offset = (lax.axis_index("query") * OWN).astype(jnp.int32).reshape(1)

    def code_of(index):
        return pl.BlockSpec(
            (1, SUBSPACES, PASSAGES), lambda s, off: (off[0] + index(s), 0, 0)
        )

    def in_order(index_of):
        return [
            index_of(lambda s: jnp.clip(2 * s - 1, 1, OWN - 1)),
            index_of(lambda s: jnp.minimum(2 * s, OWN - 1)),
        ]

    code_specs = in_order(code_of)
    table_spec = whole((CHUNKS, ENTRIES, FEATS))
    table = pltpu.VMEM((WIDTH // 128, slots, 128), F32)
    hot = pltpu.VMEM((WIDTH, PASSAGES), BF16)
    codes = (passage_codes,) * 2

    exps, message = pl.pallas_call(
        score_body,
        out_shape=(
            jax.ShapeDtypeStruct((OWN + 2, list_rows, PASSAGES), F32),
            jax.ShapeDtypeStruct((2 * devices, 128), F32),
        ),
        grid_spec=pltpu.PrefetchScalarGridSpec(
            num_scalar_prefetch=1,
            grid=(OWN // 2 + 2,),
            in_specs=[arrived, table_spec, table_spec, whole(square.shape)] + code_specs,
            out_specs=[
                pl.BlockSpec(
                    (2, list_rows, PASSAGES), lambda s, off: (jnp.maximum(s - 1, 0), 0, 0)
                ),
                whole((2 * devices, 128)),
            ],
            scratch_shapes=[table, hot, hot]
            + [pltpu.VMEM((list_rows, PASSAGES), F32)] * 2
            + [
                pltpu.VMEM(square.shape, F32),
                pltpu.VMEM((slots, D), BF16),
                pltpu.SMEM((OWN // 2,), F32),
                pltpu.SemaphoreType.DMA(()),
            ],
        ),
        compiler_params=big,
        name="score",
    )(offset, got, high, low, notes, *codes)

    message = exchange(message)
    weights = pl.pallas_call(
        weight_body,
        out_shape=square,
        scratch_shapes=[pltpu.VMEM((SLOTS, devices, count), F32)],
        name="weigh",
    )(message, masks)
    teacher = pl.pallas_call(
        teacher_body,
        out_shape=jax.ShapeDtypeStruct((OWN, list_rows, PASSAGES), F32),
        grid=(OWN,),
        in_specs=[whole((2 * devices, 128))],
        out_specs=pl.BlockSpec((1, list_rows, PASSAGES), lambda i: (i, 0, 0)),
        name="teacher",
    )(message)

    def exps_of(index):
        return pl.BlockSpec((1, list_rows, PASSAGES), lambda s, off: (index(s), 0, 0))

    result = pl.pallas_call(
        grad_body,
        out_shape=jax.ShapeDtypeStruct((devices, CHUNKS * SLOTS + BOOK_ROWS, FEATS), BF16),
        grid_spec=pltpu.PrefetchScalarGridSpec(
            num_scalar_prefetch=1,
            grid=(OWN // 2 + 1,),
            in_specs=[
                whole(square.shape),
                whole((2 * devices, 128)),
                arrived,
                table_spec,
                table_spec,
            ]
            + in_order(lambda index: exps_of(lambda s: index(s) + 1))
            + in_order(exps_of)
            + code_specs,
            out_specs=whole((devices, CHUNKS * SLOTS + BOOK_ROWS, FEATS)),
            scratch_shapes=[table, hot, hot]
            + [pltpu.VMEM((list_rows, PASSAGES), BF16)] * 2
            + [arrived_here, pltpu.SMEM((OWN // 2,), F32), pltpu.SemaphoreType.DMA((CHUNKS,))],
        ),
        compiler_params=big,
        name="grad",
    )(
        offset, uncopied(exchange(weights)), message, got, high, low,
        exps, exps, teacher, teacher, *codes,
    )

    returned = exchange(result)
    book_spec = pl.BlockSpec(
        (devices, BOOK_ROWS, FEATS), lambda b: (0, CHUNKS * SLOTS // BOOK_ROWS, 0)
    )
    book_sum = pl.pallas_call(
        book_body,
        out_shape=square,
        grid=(1,),
        in_specs=[book_spec],
        out_specs=whole(square.shape),
        name="book_sum",
    )(returned)
    normed = pl.pallas_call(
        norm_body, out_shape=jax.ShapeDtypeStruct((CENTROIDS, D), F32), name="book_norm"
    )(uncopied(exchange(book_sum)))
    grad_queries = pl.pallas_call(
        combine_body,
        out_shape=jax.ShapeDtypeStruct((count, D), BF16),
        grid=(1,),
        in_specs=[
            whole((count, slots)),
            pl.BlockSpec((devices, CHUNKS * SLOTS, FEATS), lambda b: (0, 0, 0)),
        ],
        out_specs=whole((count, D)),
        name="combine",
    )(chosen, returned)
    return grad_queries, normed


def solution(mesh):
    placed = (
        P(BOTH, None),
        P(BOTH, None),
        P(BOTH, None),
        P("corpus", None, None),
        P(),
    )

    return jax.shard_map(
        shards,
        mesh=mesh,
        in_specs=placed,
        out_specs=(P(BOTH, None), P()),
        check_vma=False,
    )
```

```python
import jax
import jax.numpy as jnp
from jax import lax
from jax.experimental import pallas as pl
from jax.experimental.pallas import tpu as pltpu
from jax.sharding import PartitionSpec as P


D = 768
SUBSPACES = 96
CENTROIDS = 16
SUBDIM = 8
PASSAGES = 1024
PROBES = 4
TARGETS = 8
CAP = 2
EPSILON = 1e-06

BOTH = ("corpus", "query")
CHUNKS = 6
FEATS = 128
ENTRIES = 256
WIDTH = SUBSPACES * CENTROIDS
OWN = 8
SLOTS = OWN * CAP
BOOK_ROWS = 8
F32 = jnp.float32
BF16 = jnp.bfloat16


def dot(a, b, dims=((1,), (0,))):
    return lax.dot_general(a, b, (dims, ((), ())), preferred_element_type=F32)


def iota(shape, axis):
    return lax.broadcasted_iota(jnp.int32, shape, axis)


def ones_where(mask):
    return jnp.where(mask, 1.0, 0.0).astype(BF16)


def split_two(value):
    high = value.astype(BF16)
    return high, (value - high.astype(F32)).astype(BF16)


def names_list(probe_rows, lists):
    found = probe_rows[0:1, :] == lists
    for p in range(1, PROBES):
        found = found | (probe_rows[p : p + 1, :] == lists)
    return found


def dispatch_body(probes_t, queries, sending, before):
    count = queries.shape[0]
    rows = sending.shape[0] // CAP
    lists = iota((rows, count), 0) + pl.program_id(0) * rows
    found = names_list(probes_t[...], lists)

    @pl.when(pl.program_id(0) == 0)
    def _():
        before[...] = ones_where(iota((count, count), 0) < iota((count, count), 1))

    rank = dot(ones_where(found), before[...])
    chosen = [
        jnp.where(found & (rank == float(r)), 1.0, 0.0).reshape(rows // OWN, 1, OWN, count)
        for r in range(CAP)
    ]
    chosen = jnp.concatenate(chosen, axis=1).reshape(rows * CAP, count).astype(BF16)
    sending[...] = dot(chosen, queries[...]).astype(BF16)


def home_body(probes_t, probes, targets_wide, chosen_out, masks_out, notes_out, used_out):
    count = probes.shape[0]
    slots = chosen_out.shape[1]
    devices = notes_out.shape[0]
    block = 512
    after = ones_where(iota((count, count), 0) > iota((count, count), 1))
    for b in range(slots // block):
        slot = iota((count, block), 1) + b * block
        lists = (slot // SLOTS) * OWN + (slot & (OWN - 1))
        found = probes[:, 0:1] == lists
        for p in range(1, PROBES):
            found = found | (probes[:, p : p + 1] == lists)
        rank = dot(after, ones_where(found))
        wanted = ((slot // OWN) & 1).astype(F32)
        chosen_out[:, b * block : (b + 1) * block] = ones_where(found & (rank == wanted))
    wide = targets_wide[...]
    spot = wide & (PASSAGES - 1)
    column = wide // PASSAGES
    in_list = jnp.broadcast_to(probes[:, 0:1], wide.shape)
    for p in range(1, PROBES):
        in_list = jnp.where(column == p, probes[:, p : p + 1], in_list)
    parts = jnp.concatenate(
        [in_list >> 5, in_list & 31, spot >> 5, spot & 31], axis=1
    ).astype(F32).astype(BF16)
    before = ones_where(iota((count, count), 0) < iota((count, count), 1))
    lane = iota((devices, 128), 1)
    gathered = jnp.zeros((devices, 4 * 128), F32)
    lane_wide = iota((devices, 4 * 128), 1) & 127
    for i in range(OWN):
        found = names_list(probes_t[...], iota((devices, count), 0) * OWN + i)
        rank = dot(ones_where(found), before)
        for r in range(CAP):
            mask = ones_where(found & (rank == float(r)))
            masks_out[r * OWN + i] = mask
            used_out[r * OWN + i] = jnp.max(mask.astype(F32)).astype(jnp.int32)
            here = dot(mask, parts)
            gathered = jnp.where(lane_wide // TARGETS == r * OWN + i, here, gathered)
    got_list = gathered[:, 0:128] * 32.0 + gathered[:, 128:256]
    got_spot = gathered[:, 256:384] * 32.0 + gathered[:, 384:512]
    own_list = iota((devices, 128), 0) * OWN + ((lane // TARGETS) & (OWN - 1))
    notes_out[...] = jnp.where(got_list == own_list.astype(F32), got_spot + 1.0, 0.0)


def fill_one_hot(codes, one_hot):
    for c in range(CHUNKS):
        part = codes[0, c * 16 : (c + 1) * 16, :].astype(F32).astype(BF16)
        for k in range(CENTROIDS):
            at = c * ENTRIES + k * 16
            one_hot[at : at + 16, :] = jnp.where(
                part == jnp.asarray(k, BF16), jnp.asarray(1, BF16), jnp.asarray(0, BF16)
            )


def score_body(
    offset, got_far, high, low, notes, odd, even,
    exps, message, table, hot_a, hot_b, held_a, held_b, stats, got, second, sem,
):
    s = pl.program_id(0)
    half = stats.shape[0]

    def score(i, hot, held, ranks):
        rows = [
            jnp.concatenate(
                [
                    table[j, pl.ds(r * OWN + i, half, stride=SLOTS), :].astype(BF16)
                    for j in range(WIDTH // 128)
                ],
                axis=1,
            )
            for r in range(ranks)
        ]
        held[0 : ranks * half, :] = dot(jnp.concatenate(rows, axis=0), hot[...])
        if ranks < CAP:
            held[ranks * half :, :] = jnp.zeros((held.shape[0] - ranks * half, PASSAGES), F32)

    def soften(i, held, place):
        scores = held[...]
        top = jnp.max(scores, axis=1, keepdims=True)
        exp_scores = jnp.exp(scores - top)
        total = jnp.sum(exp_scores, axis=1, keepdims=True)
        exps[place] = exp_scores
        lane = iota(stats.shape, 1)
        kept = stats[...]
        for r in range(CAP):
            at = r * OWN + i
            kept = jnp.where(lane == at, top[r * half : (r + 1) * half], kept)
            kept = jnp.where(lane == SLOTS + at, total[r * half : (r + 1) * half], kept)
        stats[...] = kept

    last = pl.num_programs(0) - 1

    @pl.when(s == 0)
    def _():
        copy = pltpu.make_async_copy(got_far, got, sem)
        copy.start()
        stats[...] = jnp.zeros_like(stats)
        held_b[...] = jnp.zeros_like(held_b)
        fill_one_hot(even, hot_a)
        copy.wait()
        for c in range(CHUNKS):
            rows = got[:, c * FEATS : (c + 1) * FEATS]
            twice = jnp.concatenate([rows, rows], axis=1)
            weights = jnp.concatenate([high[c], low[c]], axis=1)
            looked = dot(twice, weights, ((1,), (1,)))
            table[2 * c] = looked[:, 0:128]
            table[2 * c + 1] = looked[:, 128:256]
        size = jnp.zeros((SLOTS, FEATS), F32)
        for c in range(CHUNKS):
            rows = jnp.abs(got[:, c * FEATS : (c + 1) * FEATS])
            while rows.shape[0] > SLOTS:
                middle = rows.shape[0] // 2
                rows = jnp.maximum(rows[:middle], rows[middle:])
            size = jnp.maximum(size, rows.astype(F32))
        slot = iota(size.shape, 0)
        for pair in range(OWN // 2):
            at = OWN + 2 * pair
            second[pair] = jnp.max(jnp.where((slot == at) | (slot == at + 1), size, 0.0))

    def step(ranks):
        score(2 * s - 2, hot_a, held_a, ranks)
        fill_one_hot(odd, hot_b)
        soften(2 * s - 3, held_b, 0)
        score(2 * s - 1, hot_b, held_b, ranks)
        fill_one_hot(even, hot_a)
        soften(2 * s - 2, held_a, 1)

    inside = (s > 0) & (s < last)
    filled = second[jnp.clip(s - 1, 0, OWN // 2 - 1)] > 0.0

    @pl.when(inside & filled)
    def _():
        step(CAP)

    @pl.when(inside & jnp.logical_not(filled))
    def _():
        step(1)

    @pl.when(s == last)
    def _():
        soften(2 * s - 3, held_b, 0)
        exps[1] = jnp.zeros(exps.shape[1:], F32)
        message[...] = jnp.stack([stats[...], notes[...]], axis=1).reshape(message.shape)


def weight_body(used, stats, masks, weights, ratios, peaks, totals):
    devices, _ = masks.shape[1:]
    tops = stats[pl.ds(0, devices, stride=2), :]
    lane = iota((devices, 128), 1)

    def each_second(body):
        for s in range(OWN, SLOTS):
            pl.when(used[s] > 0)(lambda s=s: body(s))

    def top_of(s):
        return jnp.where(masks[s] > 0, tops[:, s : s + 1], -3.0e38)

    peak = top_of(0)
    for s in range(1, OWN):
        peak = jnp.maximum(peak, top_of(s))
    peaks[...] = peak

    @each_second
    def _(s):
        peaks[...] = jnp.maximum(peaks[...], top_of(s))

    peak = jnp.max(peaks[...], axis=0, keepdims=True)

    def total_of(s):
        ratio = jnp.where(masks[s] > 0, jnp.exp(tops[:, s : s + 1] - peak), 0.0)
        ratios[s] = ratio
        return ratio * tops[:, SLOTS + s : SLOTS + 1 + s]

    total = total_of(0)
    for s in range(1, OWN):
        total = total + total_of(s)
    totals[...] = total

    @each_second
    def _(s):
        totals[...] = totals[...] + total_of(s)

    share = 1.0 / jnp.sum(totals[...], axis=0, keepdims=True)
    held = jnp.zeros((devices, 128), F32)
    for s in range(OWN):
        held = jnp.where(lane == s, jnp.sum(ratios[s] * share, axis=1, keepdims=True), held)
    weights[...] = held

    @each_second
    def _(s):
        part = jnp.sum(ratios[s] * share, axis=1, keepdims=True)
        weights[...] = jnp.where(lane == s, part, weights[...])


def teacher_body(message, teacher):
    i = pl.program_id(0)
    half = message.shape[0] // 2
    turned = pltpu.roll(message[pl.ds(1, half, stride=2), :], (128 - TARGETS * i) % 128, 1)
    place = iota((half, PASSAGES), 1).astype(F32)

    def fill(r):
        held = jnp.zeros((half, PASSAGES), F32)
        for t in range(TARGETS):
            at = r * OWN * TARGETS + t
            weight = 2.0 * (TARGETS - t) / (TARGETS * (TARGETS + 1.0))
            held = jnp.where(place == turned[:, at : at + 1] - 1.0, weight, held)
        teacher[0, r * half : (r + 1) * half, :] = held

    fill(0)
    at = OWN * TARGETS
    noted = jnp.max(turned[:, at : at + TARGETS]) > 0.0

    @pl.when(noted)
    def _():
        fill(1)

    @pl.when(jnp.logical_not(noted))
    def _():
        teacher[0, half:, :] = jnp.zeros((half, PASSAGES), F32)


def grad_body(
    offset, weights, message, got_far, high, low, exps_odd, exps_even, teacher_odd, teacher_even,
    odd, even, out, hist, hot_a, hot_b, grads_a, grads_b, got, second, sems,
):
    s = pl.program_id(0)
    half = weights.shape[0]

    def prepare(i, exps, teacher, codes, hot, grads):
        lane = iota((half, 128), 1)
        for r in range(CAP):
            own = jnp.where(lane == r * OWN + i, weights[...], 0.0)
            scale = jnp.sum(own, axis=1, keepdims=True)
            rows = slice(r * half, (r + 1) * half)
            grads[rows, :] = (exps[0, rows, :] * scale - teacher[0, rows, :]).astype(BF16)
        fill_one_hot(codes, hot)

    def count(i, hot, grads, ranks):
        found = dot(grads[0 : ranks * half, :], hot[...], ((1,), (1,)))
        for r in range(ranks):
            for j in range(WIDTH // 128):
                hist[j, pl.ds(r * OWN + i, half, stride=SLOTS), :] = found[
                    r * half : (r + 1) * half, j * 128 : (j + 1) * 128
                ]

    copies = [
        pltpu.make_async_copy(got_far.at[:, c * FEATS : (c + 1) * FEATS], got.at[c], sems.at[c])
        for c in range(CHUNKS)
    ]
    following = jnp.minimum(2 * s, OWN - 1)

    @pl.when(s == 0)
    def _():
        prepare(0, exps_even, teacher_even, even, hot_a, grads_a)
        for copy in copies:
            copy.start()
        for row in range(half):
            at = row * SLOTS + OWN
            hist[:, at : at + OWN, :] = jnp.zeros((hist.shape[0], OWN, 128), F32)
        weight = jnp.max(jnp.abs(weights[...]), axis=0, keepdims=True)
        note = jnp.max(message[pl.ds(1, half, stride=2), :], axis=0, keepdims=True)
        lane = iota(weight.shape, 1)
        for pair in range(OWN // 2):
            at = OWN + 2 * pair
            held = jnp.where((lane == at) | (lane == at + 1), weight, 0.0)
            noted = jnp.where(lane // (2 * TARGETS) == at // 2, note, 0.0)
            second[pair] = jnp.maximum(jnp.max(held), jnp.max(noted))

    def step(ranks):
        count(2 * s - 2, hot_a, grads_a, ranks)
        prepare(2 * s - 1, exps_odd, teacher_odd, odd, hot_b, grads_b)
        count(2 * s - 1, hot_b, grads_b, ranks)
        prepare(following, exps_even, teacher_even, even, hot_a, grads_a)

    filled = second[jnp.maximum(s - 1, 0)] > 0.0

    @pl.when((s > 0) & filled)
    def _():
        step(CAP)

    @pl.when((s > 0) & jnp.logical_not(filled))
    def _():
        step(1)

    @pl.when(s == pl.num_programs(0) - 1)
    def _():
        for copy in copies:
            copy.wait()
        devices = out.shape[0]
        keep = iota((ENTRIES, FEATS), 0) % 16 == iota((ENTRIES, FEATS), 1) // SUBDIM
        top = CHUNKS * SLOTS
        out[CHUNKS * CENTROIDS :, top:, :] = jnp.zeros(
            (devices - CHUNKS * CENTROIDS, BOOK_ROWS, 128), BF16
        )
        for c in range(CHUNKS):
            h_high, h_low = split_two(jnp.concatenate([hist[2 * c], hist[2 * c + 1]], axis=1))
            both = jnp.concatenate([high[c], low[c]], axis=1)
            wide = dot(h_high, both)
            part = wide[:, 0:FEATS] + wide[:, FEATS:] + dot(h_low, high[c])
            out[:, c * SLOTS : (c + 1) * SLOTS, :] = part.reshape(devices, SLOTS, FEATS).astype(
                BF16
            )
            book = dot(got[c], h_high, ((0,), (0,)))
            book = jnp.where(keep, book.T, 0.0)
            book = jnp.sum(book.reshape(CENTROIDS, 16, FEATS), axis=1)
            b_high = book.astype(BF16)
            b_rest = book - b_high.astype(F32)
            b_mid = b_rest.astype(BF16)
            b_low = b_rest - b_mid.astype(F32)
            row = iota((CENTROIDS, BOOK_ROWS, FEATS), 1)
            parts = jnp.where(row == 0, b_high.astype(F32)[:, None, :], 0.0)
            parts = jnp.where(row == 1, b_mid.astype(F32)[:, None, :], parts)
            parts = jnp.where(row == 2, b_low[:, None, :], parts)
            out[c * CENTROIDS : (c + 1) * CENTROIDS, top:, :] = parts.astype(BF16)


def book_body(returned, total):
    parts = returned[...].astype(F32)
    total[...] = jnp.broadcast_to(
        jnp.sum(jnp.sum(parts, axis=0), axis=0, keepdims=True), total.shape
    )


def norm_body(rows, normed):
    value = rows[0 : CHUNKS * CENTROIDS, :]
    mean = jnp.sum(value * value, keepdims=True) / (CENTROIDS * D)
    value = value * lax.rsqrt(mean + EPSILON)
    for c in range(CHUNKS):
        normed[:, c * FEATS : (c + 1) * FEATS] = value[c * CENTROIDS : (c + 1) * CENTROIDS]


def combine_body(chosen, returned, out):
    devices = returned.shape[0]
    for c in range(CHUNKS):
        rows = returned[:, c * SLOTS : (c + 1) * SLOTS, :].reshape(devices * SLOTS, FEATS)
        out[:, c * FEATS : (c + 1) * FEATS] = dot(chosen[...], rows).astype(BF16)


def whole(shape):
    return pl.BlockSpec(shape, lambda *_: (0,) * len(shape))


def exchange(value):
    return lax.all_to_all(value, BOTH, 0, 0, tiled=True)


def uncopied(value):
    return pltpu.with_memory_space_constraint(value, pltpu.VMEM)


def spread_codebook(codebook):
    book = codebook.reshape(CENTROIDS, CHUNKS, FEATS).transpose(1, 0, 2)
    own = jnp.arange(16)[:, None] == jnp.arange(FEATS)[None, :] // SUBDIM
    spread = jnp.where(own[None, None], book[:, :, None, :], 0.0)
    spread = spread.reshape(CHUNKS, ENTRIES, FEATS)
    high = lax.reduce_precision(spread, 8, 7)
    return high.astype(BF16), (spread - high).astype(BF16)


def shards(queries, probes, targets, passage_codes, codebook):
    devices = lax.axis_size("corpus") * lax.axis_size("query")
    count = queries.shape[0]
    slots = devices * SLOTS
    list_rows = devices * CAP
    probes_t = probes.T
    big = pltpu.CompilerParams(
        dimension_semantics=("arbitrary",), vmem_limit_bytes=58 * 1024 * 1024
    )
    square = jax.ShapeDtypeStruct((devices, 128), F32)

    sending = pl.pallas_call(
        dispatch_body,
        out_shape=jax.ShapeDtypeStruct((slots, D), BF16),
        grid=(4,),
        in_specs=[whole((PROBES, count)), whole((count, D))],
        out_specs=pl.BlockSpec((slots // 4, D), lambda b: (b, 0)),
        scratch_shapes=[pltpu.VMEM((count, count), BF16)],
        name="dispatch",
    )(probes_t, queries)
    got = uncopied(exchange(sending))
    arrived = pl.BlockSpec(memory_space=pl.ANY)
    arrived_here = pltpu.VMEM((CHUNKS, slots, FEATS), BF16)

    here = pl.BlockSpec(memory_space=pltpu.VMEM)
    scalars = pl.BlockSpec(memory_space=pltpu.SMEM)
    chosen, masks, notes, used = pl.pallas_call(
        home_body,
        out_shape=(
            jax.ShapeDtypeStruct((count, slots), BF16),
            jax.ShapeDtypeStruct((SLOTS, devices, count), BF16),
            square,
            jax.ShapeDtypeStruct((SLOTS,), jnp.int32),
        ),
        out_specs=(here, here, here, scalars),
        name="home",
    )(probes_t, probes, jnp.tile(targets, (1, 128 // TARGETS)))
    high, low = spread_codebook(codebook)
    offset = (lax.axis_index("query") * OWN).astype(jnp.int32).reshape(1)

    def code_of(index):
        return pl.BlockSpec(
            (1, SUBSPACES, PASSAGES), lambda s, off: (off[0] + index(s), 0, 0)
        )

    def in_order(index_of):
        return [
            index_of(lambda s: jnp.clip(2 * s - 1, 1, OWN - 1)),
            index_of(lambda s: jnp.minimum(2 * s, OWN - 1)),
        ]

    code_specs = in_order(code_of)
    table_spec = whole((CHUNKS, ENTRIES, FEATS))
    table = pltpu.VMEM((WIDTH // 128, slots, 128), F32)
    hot = pltpu.VMEM((WIDTH, PASSAGES), BF16)
    codes = (passage_codes,) * 2

    exps, message = pl.pallas_call(
        score_body,
        out_shape=(
            jax.ShapeDtypeStruct((OWN + 2, list_rows, PASSAGES), F32),
            jax.ShapeDtypeStruct((2 * devices, 128), F32),
        ),
        grid_spec=pltpu.PrefetchScalarGridSpec(
            num_scalar_prefetch=1,
            grid=(OWN // 2 + 2,),
            in_specs=[arrived, table_spec, table_spec, whole(square.shape)] + code_specs,
            out_specs=[
                pl.BlockSpec(
                    (2, list_rows, PASSAGES), lambda s, off: (jnp.maximum(s - 1, 0), 0, 0)
                ),
                whole((2 * devices, 128)),
            ],
            scratch_shapes=[table, hot, hot]
            + [pltpu.VMEM((list_rows, PASSAGES), F32)] * 2
            + [
                pltpu.VMEM(square.shape, F32),
                pltpu.VMEM((slots, D), BF16),
                pltpu.SMEM((OWN // 2,), F32),
                pltpu.SemaphoreType.DMA(()),
            ],
        ),
        compiler_params=big,
        name="score",
    )(offset, got, high, low, notes, *codes)

    message = exchange(message)
    weights = pl.pallas_call(
        weight_body,
        out_shape=square,
        in_specs=[scalars, here, here],
        scratch_shapes=[pltpu.VMEM((SLOTS, devices, count), F32)]
        + [pltpu.VMEM((devices, count), F32)] * 2,
        name="weigh",
    )(used, message, masks)
    teacher = pl.pallas_call(
        teacher_body,
        out_shape=jax.ShapeDtypeStruct((OWN, list_rows, PASSAGES), F32),
        grid=(OWN,),
        in_specs=[whole((2 * devices, 128))],
        out_specs=pl.BlockSpec((1, list_rows, PASSAGES), lambda i: (i, 0, 0)),
        name="teacher",
    )(message)

    def exps_of(index):
        return pl.BlockSpec((1, list_rows, PASSAGES), lambda s, off: (index(s), 0, 0))

    result = pl.pallas_call(
        grad_body,
        out_shape=jax.ShapeDtypeStruct((devices, CHUNKS * SLOTS + BOOK_ROWS, FEATS), BF16),
        grid_spec=pltpu.PrefetchScalarGridSpec(
            num_scalar_prefetch=1,
            grid=(OWN // 2 + 1,),
            in_specs=[
                whole(square.shape),
                whole((2 * devices, 128)),
                arrived,
                table_spec,
                table_spec,
            ]
            + in_order(lambda index: exps_of(lambda s: index(s) + 1))
            + in_order(exps_of)
            + code_specs,
            out_specs=whole((devices, CHUNKS * SLOTS + BOOK_ROWS, FEATS)),
            scratch_shapes=[table, hot, hot]
            + [pltpu.VMEM((list_rows, PASSAGES), BF16)] * 2
            + [arrived_here, pltpu.SMEM((OWN // 2,), F32), pltpu.SemaphoreType.DMA((CHUNKS,))],
        ),
        compiler_params=big,
        name="grad",
    )(
        offset, uncopied(exchange(weights)), message, got, high, low,
        exps, exps, teacher, teacher, *codes,
    )

    returned = exchange(result)
    book_spec = pl.BlockSpec(
        (devices, BOOK_ROWS, FEATS), lambda b: (0, CHUNKS * SLOTS // BOOK_ROWS, 0)
    )
    book_sum = pl.pallas_call(
        book_body,
        out_shape=square,
        grid=(1,),
        in_specs=[book_spec],
        out_specs=whole(square.shape),
        name="book_sum",
    )(returned)
    normed = pl.pallas_call(
        norm_body, out_shape=jax.ShapeDtypeStruct((CENTROIDS, D), F32), name="book_norm"
    )(uncopied(exchange(book_sum)))
    grad_queries = pl.pallas_call(
        combine_body,
        out_shape=jax.ShapeDtypeStruct((count, D), BF16),
        grid=(1,),
        in_specs=[
            whole((count, slots)),
            pl.BlockSpec((devices, CHUNKS * SLOTS, FEATS), lambda b: (0, 0, 0)),
        ],
        out_specs=whole((count, D)),
        name="combine",
    )(chosen, returned)
    return grad_queries, normed


def solution(mesh):
    placed = (
        P(BOTH, None),
        P(BOTH, None),
        P(BOTH, None),
        P("corpus", None, None),
        P(),
    )

    return jax.shard_map(
        shards,
        mesh=mesh,
        in_specs=placed,
        out_specs=(P(BOTH, None), P()),
        check_vma=False,
    )
```

```python
import jax
import jax.numpy as jnp
from jax import lax
from jax.experimental import pallas as pl
from jax.experimental.pallas import tpu as pltpu
from jax.sharding import PartitionSpec as P


D = 768
SUBSPACES = 96
CENTROIDS = 16
SUBDIM = 8
PASSAGES = 1024
PROBES = 4
TARGETS = 8
CAP = 2
EPSILON = 1e-06

BOTH = ("corpus", "query")
CHUNKS = 6
FEATS = 128
ENTRIES = 256
WIDTH = SUBSPACES * CENTROIDS
OWN = 8
SLOTS = OWN * CAP
BOOK_ROWS = 8
F32 = jnp.float32
BF16 = jnp.bfloat16


def dot(a, b, dims=((1,), (0,))):
    return lax.dot_general(a, b, (dims, ((), ())), preferred_element_type=F32)


def iota(shape, axis):
    return lax.broadcasted_iota(jnp.int32, shape, axis)


def ones_where(mask):
    return jnp.where(mask, 1.0, 0.0).astype(BF16)


def split_two(value):
    high = value.astype(BF16)
    return high, (value - high.astype(F32)).astype(BF16)


def names_list(probe_rows, lists):
    found = probe_rows[0:1, :] == lists
    for p in range(1, PROBES):
        found = found | (probe_rows[p : p + 1, :] == lists)
    return found


def dispatch_body(probes_t, queries, sending):
    count = queries.shape[0]
    rows = sending.shape[0] // CAP
    lists = iota((rows, count), 0) + pl.program_id(0) * rows
    found = names_list(probes_t[...], lists)
    before = ones_where(iota((count, count), 0) < iota((count, count), 1))
    rank = dot(ones_where(found), before)
    chosen = [
        jnp.where(found & (rank == float(r)), 1.0, 0.0).reshape(rows // OWN, 1, OWN, count)
        for r in range(CAP)
    ]
    chosen = jnp.concatenate(chosen, axis=1).reshape(rows * CAP, count).astype(BF16)
    sending[...] = dot(chosen, queries[...]).astype(BF16)


def home_body(probes_t, probes, targets_wide, chosen_out, masks_out, notes_out, used_out):
    count = probes.shape[0]
    slots = chosen_out.shape[1]
    devices = notes_out.shape[0]
    block = 512
    after = ones_where(iota((count, count), 0) > iota((count, count), 1))
    for b in range(slots // block):
        slot = iota((count, block), 1) + b * block
        lists = (slot // SLOTS) * OWN + (slot & (OWN - 1))
        found = probes[:, 0:1] == lists
        for p in range(1, PROBES):
            found = found | (probes[:, p : p + 1] == lists)
        rank = dot(after, ones_where(found))
        wanted = ((slot // OWN) & 1).astype(F32)
        chosen_out[:, b * block : (b + 1) * block] = ones_where(found & (rank == wanted))
    wide = targets_wide[...]
    spot = wide & (PASSAGES - 1)
    column = wide // PASSAGES
    in_list = jnp.broadcast_to(probes[:, 0:1], wide.shape)
    for p in range(1, PROBES):
        in_list = jnp.where(column == p, probes[:, p : p + 1], in_list)
    parts = jnp.concatenate(
        [in_list >> 5, in_list & 31, spot >> 5, spot & 31], axis=1
    ).astype(F32).astype(BF16)
    before = ones_where(iota((count, count), 0) < iota((count, count), 1))
    lane = iota((devices, 128), 1)
    gathered = jnp.zeros((devices, 4 * 128), F32)
    lane_wide = iota((devices, 4 * 128), 1) & 127
    for i in range(OWN):
        found = names_list(probes_t[...], iota((devices, count), 0) * OWN + i)
        rank = dot(ones_where(found), before)
        for r in range(CAP):
            mask = ones_where(found & (rank == float(r)))
            masks_out[r * OWN + i] = mask
            used_out[r * OWN + i] = jnp.max(mask.astype(F32)).astype(jnp.int32)
            here = dot(mask, parts)
            gathered = jnp.where(lane_wide // TARGETS == r * OWN + i, here, gathered)
    got_list = gathered[:, 0:128] * 32.0 + gathered[:, 128:256]
    got_spot = gathered[:, 256:384] * 32.0 + gathered[:, 384:512]
    own_list = iota((devices, 128), 0) * OWN + ((lane // TARGETS) & (OWN - 1))
    notes_out[...] = jnp.where(got_list == own_list.astype(F32), got_spot + 1.0, 0.0)


def fill_one_hot(codes, one_hot):
    for c in range(CHUNKS):
        part = codes[0, c * 16 : (c + 1) * 16, :].astype(F32).astype(BF16)
        for k in range(CENTROIDS):
            at = c * ENTRIES + k * 16
            one_hot[at : at + 16, :] = jnp.where(
                part == jnp.asarray(k, BF16), jnp.asarray(1, BF16), jnp.asarray(0, BF16)
            )


def score_body(
    offset, got_far, high, low, notes, odd, even,
    exps, message, table, hot_a, hot_b, held_a, held_b, stats, got, second, sem,
):
    s = pl.program_id(0)
    half = stats.shape[0]

    def score(i, hot, held, ranks):
        rows = [
            jnp.concatenate(
                [
                    table[j, pl.ds(r * OWN + i, half, stride=SLOTS), :].astype(BF16)
                    for j in range(WIDTH // 128)
                ],
                axis=1,
            )
            for r in range(ranks)
        ]
        held[0 : ranks * half, :] = dot(jnp.concatenate(rows, axis=0), hot[...])
        if ranks < CAP:
            held[ranks * half :, :] = jnp.zeros((held.shape[0] - ranks * half, PASSAGES), F32)

    def soften(i, held, place):
        scores = held[...]
        top = jnp.max(scores, axis=1, keepdims=True)
        exp_scores = jnp.exp(scores - top)
        total = jnp.sum(exp_scores, axis=1, keepdims=True)
        exps[place] = exp_scores
        lane = iota(stats.shape, 1)
        kept = stats[...]
        for r in range(CAP):
            at = r * OWN + i
            kept = jnp.where(lane == at, top[r * half : (r + 1) * half], kept)
            kept = jnp.where(lane == SLOTS + at, total[r * half : (r + 1) * half], kept)
        stats[...] = kept

    last = pl.num_programs(0) - 1

    @pl.when(s == 0)
    def _():
        copy = pltpu.make_async_copy(got_far, got, sem)
        copy.start()
        stats[...] = jnp.zeros_like(stats)
        held_b[...] = jnp.zeros_like(held_b)
        fill_one_hot(even, hot_a)
        copy.wait()
        for c in range(CHUNKS):
            rows = got[:, c * FEATS : (c + 1) * FEATS]
            twice = jnp.concatenate([rows, rows], axis=1)
            weights = jnp.concatenate([high[c], low[c]], axis=1)
            looked = dot(twice, weights, ((1,), (1,)))
            table[2 * c] = looked[:, 0:128]
            table[2 * c + 1] = looked[:, 128:256]
        size = jnp.zeros((SLOTS, FEATS), F32)
        for c in range(CHUNKS):
            rows = jnp.abs(got[:, c * FEATS : (c + 1) * FEATS])
            while rows.shape[0] > SLOTS:
                middle = rows.shape[0] // 2
                rows = jnp.maximum(rows[:middle], rows[middle:])
            size = jnp.maximum(size, rows.astype(F32))
        slot = iota(size.shape, 0)
        for pair in range(OWN // 2):
            at = OWN + 2 * pair
            second[pair] = jnp.max(jnp.where((slot == at) | (slot == at + 1), size, 0.0))

    def step(ranks):
        score(2 * s - 2, hot_a, held_a, ranks)
        fill_one_hot(odd, hot_b)
        soften(2 * s - 3, held_b, 0)
        score(2 * s - 1, hot_b, held_b, ranks)
        fill_one_hot(even, hot_a)
        soften(2 * s - 2, held_a, 1)

    inside = (s > 0) & (s < last)
    filled = second[jnp.clip(s - 1, 0, OWN // 2 - 1)] > 0.0

    @pl.when(inside & filled)
    def _():
        step(CAP)

    @pl.when(inside & jnp.logical_not(filled))
    def _():
        step(1)

    @pl.when(s == last)
    def _():
        soften(2 * s - 3, held_b, 0)
        exps[1] = jnp.zeros(exps.shape[1:], F32)
        message[...] = jnp.stack([stats[...], notes[...]], axis=1).reshape(message.shape)


def weight_body(used, stats, masks, weights, ratios, peaks, totals):
    devices, _ = masks.shape[1:]
    tops = stats[pl.ds(0, devices, stride=2), :]
    lane = iota((devices, 128), 1)

    def each_second(body):
        for s in range(OWN, SLOTS):
            pl.when(used[s] > 0)(lambda s=s: body(s))

    def top_of(s):
        return jnp.where(masks[s] > 0, tops[:, s : s + 1], -3.0e38)

    peak = top_of(0)
    for s in range(1, OWN):
        peak = jnp.maximum(peak, top_of(s))
    peaks[...] = peak

    @each_second
    def _(s):
        peaks[...] = jnp.maximum(peaks[...], top_of(s))

    peak = jnp.max(peaks[...], axis=0, keepdims=True)

    def total_of(s):
        ratio = jnp.where(masks[s] > 0, jnp.exp(tops[:, s : s + 1] - peak), 0.0)
        ratios[s] = ratio
        return ratio * tops[:, SLOTS + s : SLOTS + 1 + s]

    total = total_of(0)
    for s in range(1, OWN):
        total = total + total_of(s)
    totals[...] = total

    @each_second
    def _(s):
        totals[...] = totals[...] + total_of(s)

    share = 1.0 / jnp.sum(totals[...], axis=0, keepdims=True)
    held = jnp.zeros((devices, 128), F32)
    for s in range(OWN):
        held = jnp.where(lane == s, jnp.sum(ratios[s] * share, axis=1, keepdims=True), held)
    weights[...] = held

    @each_second
    def _(s):
        part = jnp.sum(ratios[s] * share, axis=1, keepdims=True)
        weights[...] = jnp.where(lane == s, part, weights[...])


def teacher_body(message, teacher):
    i = pl.program_id(0)
    half = message.shape[0] // 2
    turned = pltpu.roll(message[pl.ds(1, half, stride=2), :], (128 - TARGETS * i) % 128, 1)
    place = iota((half, PASSAGES), 1).astype(F32)

    def fill(r):
        held = jnp.zeros((half, PASSAGES), F32)
        for t in range(TARGETS):
            at = r * OWN * TARGETS + t
            weight = 2.0 * (TARGETS - t) / (TARGETS * (TARGETS + 1.0))
            held = jnp.where(place == turned[:, at : at + 1] - 1.0, weight, held)
        teacher[0, r * half : (r + 1) * half, :] = held

    fill(0)
    at = OWN * TARGETS
    noted = jnp.max(turned[:, at : at + TARGETS]) > 0.0

    @pl.when(noted)
    def _():
        fill(1)

    @pl.when(jnp.logical_not(noted))
    def _():
        teacher[0, half:, :] = jnp.zeros((half, PASSAGES), F32)


def regroup_body(got, rows):
    size = got.shape[0]
    row, column = iota((size, size), 0), iota((size, size), 1)
    turn = ones_where((row // SLOTS == column % SLOTS) & (row % SLOTS == column // SLOTS))
    turned = dot(turn, got[...]).astype(BF16)
    for slot in range(SLOTS):
        rows[slot] = turned[slot * SLOTS : (slot + 1) * SLOTS, :]


def grad_body(
    offset, weights, message, got_far, high, low, exps_odd, exps_even, teacher_odd, teacher_even,
    odd, even, out, hist, hot_a, hot_b, grads_a, grads_b, got, second,
    spread, books, sems,
):
    s = pl.program_id(0)
    half = weights.shape[0]

    def prepare(i, exps, teacher, codes, hot, grads):
        lane = iota((half, 128), 1)
        for r in range(CAP):
            own = jnp.where(lane == r * OWN + i, weights[...], 0.0)
            scale = jnp.sum(own, axis=1, keepdims=True)
            rows = slice(r * half, (r + 1) * half)
            grads[rows, :] = (exps[0, rows, :] * scale - teacher[0, rows, :]).astype(BF16)
        fill_one_hot(codes, hot)

    def count(i, hot, grads, ranks):
        found = dot(grads[0 : ranks * half, :], hot[...], ((1,), (1,)))
        for r in range(ranks):
            for j in range(WIDTH // 128):
                at = pl.multiple_of((r * OWN + i) * half, half)
                hist[j, pl.ds(at, half), :] = found[
                    r * half : (r + 1) * half, j * 128 : (j + 1) * 128
                ]

    copies = [
        pltpu.make_async_copy(got_far.at[:, c * FEATS : (c + 1) * FEATS], got.at[c], sems.at[c])
        for c in range(CHUNKS)
    ]
    following = jnp.minimum(2 * s, OWN - 1)

    @pl.when(s == 0)
    def _():
        prepare(0, exps_even, teacher_even, even, hot_a, grads_a)
        for copy in copies:
            copy.start()
        for row in range(half):
            at = row * SLOTS + OWN
            spread[:, at : at + OWN, :] = jnp.zeros((CHUNKS, OWN, FEATS), F32)
        weight = jnp.max(jnp.abs(weights[...]), axis=0, keepdims=True)
        note = jnp.max(message[pl.ds(1, half, stride=2), :], axis=0, keepdims=True)
        lane = iota(weight.shape, 1)
        for pair in range(OWN // 2):
            at = OWN + 2 * pair
            held = jnp.where((lane == at) | (lane == at + 1), weight, 0.0)
            noted = jnp.where(lane // (2 * TARGETS) == at // 2, note, 0.0)
            second[pair] = jnp.maximum(jnp.max(held), jnp.max(noted))

    def step(ranks):
        count(2 * s - 2, hot_a, grads_a, ranks)
        prepare(2 * s - 1, exps_odd, teacher_odd, odd, hot_b, grads_b)
        count(2 * s - 1, hot_b, grads_b, ranks)
        prepare(following, exps_even, teacher_even, even, hot_a, grads_a)

    filled = second[jnp.maximum(s - 1, 0)] > 0.0

    @pl.when((s > 0) & filled)
    def _():
        step(CAP)

    @pl.when((s > 0) & jnp.logical_not(filled))
    def _():
        step(1)

    last = s == pl.num_programs(0) - 1

    def finish(slot, slots):
        rows = slice(slot * half, (slot + slots) * half)
        for c in range(CHUNKS):
            h_high, h_low = split_two(
                jnp.concatenate([hist[2 * c, rows, :], hist[2 * c + 1, rows, :]], axis=1)
            )
            both = jnp.concatenate([high[c], low[c]], axis=1)
            wide = dot(h_high, both)
            part = wide[:, 0:FEATS] + wide[:, FEATS:] + dot(h_low, high[c])
            for j in range(slots):
                spread[c, pl.ds(slot + j, half, stride=SLOTS), :] = part[j * half : (j + 1) * half]
            book = dot(got[c, rows, :], h_high, ((0,), (0,)))
            books[c] = book if slot == 0 else books[c] + book

    @pl.when(last)
    def _():
        for copy in copies:
            copy.wait()
        finish(0, OWN)

    for pair in range(OWN // 2):

        @pl.when(last & (second[pair] > 0.0))
        def _(pair=pair):
            finish(OWN + 2 * pair, 2)

    @pl.when(last)
    def _():
        devices = out.shape[0]
        keep = iota((ENTRIES, FEATS), 0) % 16 == iota((ENTRIES, FEATS), 1) // SUBDIM
        top = CHUNKS * SLOTS
        out[CHUNKS * CENTROIDS :, top:, :] = jnp.zeros(
            (devices - CHUNKS * CENTROIDS, BOOK_ROWS, 128), BF16
        )
        for c in range(CHUNKS):
            part = spread[c].reshape(devices, SLOTS, FEATS)
            out[:, c * SLOTS : (c + 1) * SLOTS, :] = part.astype(BF16)
            book = jnp.where(keep, books[c].T, 0.0)
            book = jnp.sum(book.reshape(CENTROIDS, 16, FEATS), axis=1)
            b_high = book.astype(BF16)
            b_rest = book - b_high.astype(F32)
            b_mid = b_rest.astype(BF16)
            b_low = b_rest - b_mid.astype(F32)
            row = iota((CENTROIDS, BOOK_ROWS, FEATS), 1)
            parts = jnp.where(row == 0, b_high.astype(F32)[:, None, :], 0.0)
            parts = jnp.where(row == 1, b_mid.astype(F32)[:, None, :], parts)
            parts = jnp.where(row == 2, b_low[:, None, :], parts)
            out[c * CENTROIDS : (c + 1) * CENTROIDS, top:, :] = parts.astype(BF16)


def book_body(returned, total):
    parts = returned[...].astype(F32)
    total[...] = jnp.broadcast_to(
        jnp.sum(jnp.sum(parts, axis=0), axis=0, keepdims=True), total.shape
    )


def norm_body(rows, normed):
    value = rows[0 : CHUNKS * CENTROIDS, :]
    mean = jnp.sum(value * value, keepdims=True) / (CENTROIDS * D)
    value = value * lax.rsqrt(mean + EPSILON)
    for c in range(CHUNKS):
        normed[:, c * FEATS : (c + 1) * FEATS] = value[c * CENTROIDS : (c + 1) * CENTROIDS]


def combine_body(chosen, returned, out):
    devices = returned.shape[0]
    for c in range(CHUNKS):
        rows = returned[:, c * SLOTS : (c + 1) * SLOTS, :].reshape(devices * SLOTS, FEATS)
        out[:, c * FEATS : (c + 1) * FEATS] = dot(chosen[...], rows).astype(BF16)


def whole(shape):
    return pl.BlockSpec(shape, lambda *_: (0,) * len(shape))


def exchange(value):
    return lax.all_to_all(value, BOTH, 0, 0, tiled=True)


def uncopied(value):
    return pltpu.with_memory_space_constraint(value, pltpu.VMEM)


def spread_codebook(codebook):
    book = codebook.reshape(CENTROIDS, CHUNKS, FEATS).transpose(1, 0, 2)
    own = jnp.arange(16)[:, None] == jnp.arange(FEATS)[None, :] // SUBDIM
    spread = jnp.where(own[None, None], book[:, :, None, :], 0.0)
    spread = spread.reshape(CHUNKS, ENTRIES, FEATS)
    high = lax.reduce_precision(spread, 8, 7)
    return high.astype(BF16), (spread - high).astype(BF16)


def shards(queries, probes, targets, passage_codes, codebook):
    devices = lax.axis_size("corpus") * lax.axis_size("query")
    count = queries.shape[0]
    slots = devices * SLOTS
    list_rows = devices * CAP
    probes_t = probes.T
    big = pltpu.CompilerParams(
        dimension_semantics=("arbitrary",), vmem_limit_bytes=58 * 1024 * 1024
    )
    square = jax.ShapeDtypeStruct((devices, 128), F32)

    sending = pl.pallas_call(
        dispatch_body,
        out_shape=jax.ShapeDtypeStruct((slots, D), BF16),
        grid=(4,),
        in_specs=[whole((PROBES, count)), whole((count, D))],
        out_specs=pl.BlockSpec((slots // 4, D), lambda b: (b, 0)),
        name="dispatch",
    )(probes_t, queries)
    got = uncopied(exchange(sending))
    arrived = pl.BlockSpec(memory_space=pl.ANY)
    arrived_here = pltpu.VMEM((CHUNKS, slots, FEATS), BF16)

    here = pl.BlockSpec(memory_space=pltpu.VMEM)
    scalars = pl.BlockSpec(memory_space=pltpu.SMEM)
    chosen, masks, notes, used = pl.pallas_call(
        home_body,
        out_shape=(
            jax.ShapeDtypeStruct((count, slots), BF16),
            jax.ShapeDtypeStruct((SLOTS, devices, count), BF16),
            square,
            jax.ShapeDtypeStruct((SLOTS,), jnp.int32),
        ),
        out_specs=(here, here, here, scalars),
        name="home",
    )(probes_t, probes, jnp.tile(targets, (1, 128 // TARGETS)))
    high, low = spread_codebook(codebook)
    offset = (lax.axis_index("query") * OWN).astype(jnp.int32).reshape(1)

    def code_of(index):
        return pl.BlockSpec(
            (1, SUBSPACES, PASSAGES), lambda s, off: (off[0] + index(s), 0, 0)
        )

    def in_order(index_of):
        return [
            index_of(lambda s: jnp.clip(2 * s - 1, 1, OWN - 1)),
            index_of(lambda s: jnp.minimum(2 * s, OWN - 1)),
        ]

    code_specs = in_order(code_of)
    table_spec = whole((CHUNKS, ENTRIES, FEATS))
    table = pltpu.VMEM((WIDTH // 128, slots, 128), F32)
    hot = pltpu.VMEM((WIDTH, PASSAGES), BF16)
    codes = (passage_codes,) * 2

    exps, message = pl.pallas_call(
        score_body,
        out_shape=(
            jax.ShapeDtypeStruct((OWN + 2, list_rows, PASSAGES), F32),
            jax.ShapeDtypeStruct((2 * devices, 128), F32),
        ),
        grid_spec=pltpu.PrefetchScalarGridSpec(
            num_scalar_prefetch=1,
            grid=(OWN // 2 + 2,),
            in_specs=[arrived, table_spec, table_spec, whole(square.shape)] + code_specs,
            out_specs=[
                pl.BlockSpec(
                    (2, list_rows, PASSAGES), lambda s, off: (jnp.maximum(s - 1, 0), 0, 0)
                ),
                whole((2 * devices, 128)),
            ],
            scratch_shapes=[table, hot, hot]
            + [pltpu.VMEM((list_rows, PASSAGES), F32)] * 2
            + [
                pltpu.VMEM(square.shape, F32),
                pltpu.VMEM((slots, D), BF16),
                pltpu.SMEM((OWN // 2,), F32),
                pltpu.SemaphoreType.DMA(()),
            ],
        ),
        compiler_params=big,
        name="score",
    )(offset, got, high, low, notes, *codes)

    message = uncopied(exchange(message))
    regrouped = pl.pallas_call(
        regroup_body,
        out_shape=jax.ShapeDtypeStruct((SLOTS, devices, D), BF16),
        grid=(devices // SLOTS,),
        in_specs=[pl.BlockSpec((SLOTS * SLOTS, D), lambda b: (b, 0))],
        out_specs=pl.BlockSpec((SLOTS, SLOTS, D), lambda b: (0, b, 0)),
        name="regroup",
    )(got).reshape(slots, D)
    weights = pl.pallas_call(
        weight_body,
        out_shape=square,
        in_specs=[scalars, here, here],
        scratch_shapes=[pltpu.VMEM((SLOTS, devices, count), F32)]
        + [pltpu.VMEM((devices, count), F32)] * 2,
        name="weigh",
    )(used, message, masks)
    teacher = pl.pallas_call(
        teacher_body,
        out_shape=jax.ShapeDtypeStruct((OWN, list_rows, PASSAGES), F32),
        grid=(OWN,),
        in_specs=[whole((2 * devices, 128))],
        out_specs=pl.BlockSpec((1, list_rows, PASSAGES), lambda i: (i, 0, 0)),
        name="teacher",
    )(message)

    def exps_of(index):
        return pl.BlockSpec((1, list_rows, PASSAGES), lambda s, off: (index(s), 0, 0))

    result = pl.pallas_call(
        grad_body,
        out_shape=jax.ShapeDtypeStruct((devices, CHUNKS * SLOTS + BOOK_ROWS, FEATS), BF16),
        grid_spec=pltpu.PrefetchScalarGridSpec(
            num_scalar_prefetch=1,
            grid=(OWN // 2 + 1,),
            in_specs=[
                whole(square.shape),
                whole((2 * devices, 128)),
                arrived,
                table_spec,
                table_spec,
            ]
            + in_order(lambda index: exps_of(lambda s: index(s) + 1))
            + in_order(exps_of)
            + code_specs,
            out_specs=whole((devices, CHUNKS * SLOTS + BOOK_ROWS, FEATS)),
            scratch_shapes=[table, hot, hot]
            + [pltpu.VMEM((list_rows, PASSAGES), BF16)] * 2
            + [
                arrived_here,
                pltpu.SMEM((OWN // 2,), F32),
                pltpu.VMEM((CHUNKS, slots, FEATS), F32),
                pltpu.VMEM((CHUNKS, FEATS, ENTRIES), F32),
                pltpu.SemaphoreType.DMA((CHUNKS,)),
            ],
        ),
        compiler_params=big,
        name="grad",
    )(
        offset, uncopied(exchange(weights)), message, regrouped, high, low,
        exps, exps, teacher, teacher, *codes,
    )

    returned = exchange(result)
    book_spec = pl.BlockSpec(
        (devices, BOOK_ROWS, FEATS), lambda b: (0, CHUNKS * SLOTS // BOOK_ROWS, 0)
    )
    book_sum = pl.pallas_call(
        book_body,
        out_shape=square,
        grid=(1,),
        in_specs=[book_spec],
        out_specs=whole(square.shape),
        name="book_sum",
    )(returned)
    normed = pl.pallas_call(
        norm_body, out_shape=jax.ShapeDtypeStruct((CENTROIDS, D), F32), name="book_norm"
    )(uncopied(exchange(book_sum)))
    grad_queries = pl.pallas_call(
        combine_body,
        out_shape=jax.ShapeDtypeStruct((count, D), BF16),
        grid=(1,),
        in_specs=[
            whole((count, slots)),
            pl.BlockSpec((devices, CHUNKS * SLOTS, FEATS), lambda b: (0, 0, 0)),
        ],
        out_specs=whole((count, D)),
        name="combine",
    )(chosen, returned)
    return grad_queries, normed


def solution(mesh):
    placed = (
        P(BOTH, None),
        P(BOTH, None),
        P(BOTH, None),
        P("corpus", None, None),
        P(),
    )

    return jax.shard_map(
        shards,
        mesh=mesh,
        in_specs=placed,
        out_specs=(P(BOTH, None), P()),
        check_vma=False,
    )
```

```python
import jax
import jax.numpy as jnp
from jax import lax
from jax.experimental import pallas as pl
from jax.experimental.pallas import tpu as pltpu
from jax.sharding import PartitionSpec as P


D = 768
SUBSPACES = 96
CENTROIDS = 16
SUBDIM = 8
PASSAGES = 1024
PROBES = 4
TARGETS = 8
CAP = 2
EPSILON = 1e-06

BOTH = ("corpus", "query")
CHUNKS = 6
FEATS = 128
ENTRIES = 256
WIDTH = SUBSPACES * CENTROIDS
OWN = 8
SLOTS = OWN * CAP
BOOK_ROWS = 8
F32 = jnp.float32
BF16 = jnp.bfloat16


def dot(a, b, dims=((1,), (0,))):
    return lax.dot_general(a, b, (dims, ((), ())), preferred_element_type=F32)


def iota(shape, axis):
    return lax.broadcasted_iota(jnp.int32, shape, axis)


def ones_where(mask):
    return jnp.where(mask, 1.0, 0.0).astype(BF16)


def split_two(value):
    high = value.astype(BF16)
    return high, (value - high.astype(F32)).astype(BF16)


def names_list(probe_rows, lists):
    found = probe_rows[0:1, :] == lists
    for p in range(1, PROBES):
        found = found | (probe_rows[p : p + 1, :] == lists)
    return found


def dispatch_body(probes_t, queries, sending):
    count = queries.shape[0]
    rows = sending.shape[0] // CAP
    lists = iota((rows, count), 0) + pl.program_id(0) * rows
    found = names_list(probes_t[...], lists)
    before = ones_where(iota((count, count), 0) < iota((count, count), 1))
    rank = dot(ones_where(found), before)
    chosen = [
        jnp.where(found & (rank == float(r)), 1.0, 0.0).reshape(rows // OWN, 1, OWN, count)
        for r in range(CAP)
    ]
    chosen = jnp.concatenate(chosen, axis=1).reshape(rows * CAP, count).astype(BF16)
    sending[...] = dot(chosen, queries[...]).astype(BF16)


def home_body(probes_t, probes, targets_wide, chosen_out, masks_out, notes_out, used_out):
    count = probes.shape[0]
    slots = chosen_out.shape[1]
    devices = notes_out.shape[0]
    block = 512
    after = ones_where(iota((count, count), 0) > iota((count, count), 1))
    for b in range(slots // block):
        slot = iota((count, block), 1) + b * block
        lists = (slot // SLOTS) * OWN + (slot & (OWN - 1))
        found = probes[:, 0:1] == lists
        for p in range(1, PROBES):
            found = found | (probes[:, p : p + 1] == lists)
        rank = dot(after, ones_where(found))
        wanted = ((slot // OWN) & 1).astype(F32)
        chosen_out[:, b * block : (b + 1) * block] = ones_where(found & (rank == wanted))
    wide = targets_wide[...]
    spot = wide & (PASSAGES - 1)
    column = wide // PASSAGES
    in_list = jnp.broadcast_to(probes[:, 0:1], wide.shape)
    for p in range(1, PROBES):
        in_list = jnp.where(column == p, probes[:, p : p + 1], in_list)
    parts = jnp.concatenate(
        [in_list >> 5, in_list & 31, spot >> 5, spot & 31], axis=1
    ).astype(F32).astype(BF16)
    before = ones_where(iota((count, count), 0) < iota((count, count), 1))
    lane = iota((devices, 128), 1)
    gathered = jnp.zeros((devices, 4 * 128), F32)
    lane_wide = iota((devices, 4 * 128), 1) & 127
    for i in range(OWN):
        found = names_list(probes_t[...], iota((devices, count), 0) * OWN + i)
        rank = dot(ones_where(found), before)
        for r in range(CAP):
            mask = ones_where(found & (rank == float(r)))
            masks_out[r * OWN + i] = mask
            used_out[r * OWN + i] = jnp.max(mask.astype(F32)).astype(jnp.int32)
            here = dot(mask, parts)
            gathered = jnp.where(lane_wide // TARGETS == r * OWN + i, here, gathered)
    got_list = gathered[:, 0:128] * 32.0 + gathered[:, 128:256]
    got_spot = gathered[:, 256:384] * 32.0 + gathered[:, 384:512]
    own_list = iota((devices, 128), 0) * OWN + ((lane // TARGETS) & (OWN - 1))
    notes_out[...] = jnp.where(got_list == own_list.astype(F32), got_spot + 1.0, 0.0)


def fill_one_hot(codes, one_hot):
    for c in range(CHUNKS):
        part = codes[0, c * 16 : (c + 1) * 16, :].astype(F32).astype(BF16)
        for k in range(CENTROIDS):
            at = c * ENTRIES + k * 16
            one_hot[at : at + 16, :] = jnp.where(
                part == jnp.asarray(k, BF16), jnp.asarray(1, BF16), jnp.asarray(0, BF16)
            )


def score_body(
    offset, got_far, high, low, notes, odd, even,
    exps, message, table, hot_a, hot_b, held_a, held_b, stats, got, second, sem,
):
    s = pl.program_id(0)
    half = stats.shape[0]

    def score(i, hot, held, ranks):
        rows = [
            jnp.concatenate(
                [
                    table[j, pl.ds(r * OWN + i, half, stride=SLOTS), :].astype(BF16)
                    for j in range(WIDTH // 128)
                ],
                axis=1,
            )
            for r in range(ranks)
        ]
        held[0 : ranks * half, :] = dot(jnp.concatenate(rows, axis=0), hot[...])
        if ranks < CAP:
            held[ranks * half :, :] = jnp.zeros((held.shape[0] - ranks * half, PASSAGES), F32)

    def soften(i, held, place):
        scores = held[...]
        top = jnp.max(scores, axis=1, keepdims=True)
        exp_scores = jnp.exp(scores - top)
        total = jnp.sum(exp_scores, axis=1, keepdims=True)
        exps[place] = exp_scores
        lane = iota(stats.shape, 1)
        kept = stats[...]
        for r in range(CAP):
            at = r * OWN + i
            kept = jnp.where(lane == at, top[r * half : (r + 1) * half], kept)
            kept = jnp.where(lane == SLOTS + at, total[r * half : (r + 1) * half], kept)
        stats[...] = kept

    last = pl.num_programs(0) - 1

    @pl.when(s == 0)
    def _():
        copy = pltpu.make_async_copy(got_far, got, sem)
        copy.start()
        stats[...] = jnp.zeros_like(stats)
        held_b[...] = jnp.zeros_like(held_b)
        fill_one_hot(even, hot_a)
        copy.wait()
        for c in range(CHUNKS):
            rows = got[:, c * FEATS : (c + 1) * FEATS]
            twice = jnp.concatenate([rows, rows], axis=1)
            weights = jnp.concatenate([high[c], low[c]], axis=1)
            looked = dot(twice, weights, ((1,), (1,)))
            table[2 * c] = looked[:, 0:128]
            table[2 * c + 1] = looked[:, 128:256]
        size = jnp.zeros((SLOTS, FEATS), F32)
        for c in range(CHUNKS):
            rows = jnp.abs(got[:, c * FEATS : (c + 1) * FEATS])
            while rows.shape[0] > SLOTS:
                middle = rows.shape[0] // 2
                rows = jnp.maximum(rows[:middle], rows[middle:])
            size = jnp.maximum(size, rows.astype(F32))
        slot = iota(size.shape, 0)
        for pair in range(OWN // 2):
            at = OWN + 2 * pair
            second[pair] = jnp.max(jnp.where((slot == at) | (slot == at + 1), size, 0.0))

    def step(ranks):
        score(2 * s - 2, hot_a, held_a, ranks)
        fill_one_hot(odd, hot_b)
        soften(2 * s - 3, held_b, 0)
        score(2 * s - 1, hot_b, held_b, ranks)
        fill_one_hot(even, hot_a)
        soften(2 * s - 2, held_a, 1)

    inside = (s > 0) & (s < last)
    filled = second[jnp.clip(s - 1, 0, OWN // 2 - 1)] > 0.0

    @pl.when(inside & filled)
    def _():
        step(CAP)

    @pl.when(inside & jnp.logical_not(filled))
    def _():
        step(1)

    @pl.when(s == last)
    def _():
        soften(2 * s - 3, held_b, 0)
        exps[1] = jnp.zeros(exps.shape[1:], F32)
        message[...] = jnp.stack([stats[...], notes[...]], axis=1).reshape(message.shape)


def weight_body(used, stats, masks, weights, ratios, peaks, totals):
    devices, _ = masks.shape[1:]
    tops = stats[pl.ds(0, devices, stride=2), :]
    lane = iota((devices, 128), 1)

    def each_second(body):
        for s in range(OWN, SLOTS):
            pl.when(used[s] > 0)(lambda s=s: body(s))

    def top_of(s):
        return jnp.where(masks[s] > 0, tops[:, s : s + 1], -3.0e38)

    peak = top_of(0)
    for s in range(1, OWN):
        peak = jnp.maximum(peak, top_of(s))
    peaks[...] = peak

    @each_second
    def _(s):
        peaks[...] = jnp.maximum(peaks[...], top_of(s))

    peak = jnp.max(peaks[...], axis=0, keepdims=True)

    def total_of(s):
        ratio = jnp.where(masks[s] > 0, jnp.exp(tops[:, s : s + 1] - peak), 0.0)
        ratios[s] = ratio
        return ratio * tops[:, SLOTS + s : SLOTS + 1 + s]

    total = total_of(0)
    for s in range(1, OWN):
        total = total + total_of(s)
    totals[...] = total

    @each_second
    def _(s):
        totals[...] = totals[...] + total_of(s)

    share = 1.0 / jnp.sum(totals[...], axis=0, keepdims=True)
    held = jnp.zeros((devices, 128), F32)
    for s in range(OWN):
        held = jnp.where(lane == s, jnp.sum(ratios[s] * share, axis=1, keepdims=True), held)
    weights[...] = held

    @each_second
    def _(s):
        part = jnp.sum(ratios[s] * share, axis=1, keepdims=True)
        weights[...] = jnp.where(lane == s, part, weights[...])


def teacher_body(message, teacher):
    i = pl.program_id(0)
    half = message.shape[0] // 2
    turned = pltpu.roll(message[pl.ds(1, half, stride=2), :], (128 - TARGETS * i) % 128, 1)
    place = iota((half, PASSAGES), 1).astype(F32)

    def fill(r):
        held = jnp.zeros((half, PASSAGES), F32)
        for t in range(TARGETS):
            at = r * OWN * TARGETS + t
            weight = 2.0 * (TARGETS - t) / (TARGETS * (TARGETS + 1.0))
            held = jnp.where(place == turned[:, at : at + 1] - 1.0, weight, held)
        teacher[0, r * half : (r + 1) * half, :] = held

    fill(0)
    at = OWN * TARGETS
    noted = jnp.max(turned[:, at : at + TARGETS]) > 0.0

    @pl.when(noted)
    def _():
        fill(1)

    @pl.when(jnp.logical_not(noted))
    def _():
        teacher[0, half:, :] = jnp.zeros((half, PASSAGES), F32)


def regroup_body(got, rows):
    size = got.shape[0]
    row, column = iota((size, size), 0), iota((size, size), 1)
    turn = ones_where((row // SLOTS == column % SLOTS) & (row % SLOTS == column // SLOTS))
    turned = dot(turn, got[...]).astype(BF16)
    for slot in range(SLOTS):
        rows[slot] = turned[slot * SLOTS : (slot + 1) * SLOTS, :]


def grad_body(
    offset, weights, message, got_far, high, low, exps_odd, exps_even, teacher_odd, teacher_even,
    odd, even, out, hist, hot_a, hot_b, grads_a, grads_b, got, second,
    spread, books, sems,
):
    s = pl.program_id(0)
    half = weights.shape[0]

    def prepare(i, exps, teacher, codes, hot, grads):
        lane = iota((half, 128), 1)
        for r in range(CAP):
            own = jnp.where(lane == r * OWN + i, weights[...], 0.0)
            scale = jnp.sum(own, axis=1, keepdims=True)
            rows = slice(r * half, (r + 1) * half)
            grads[rows, :] = (exps[0, rows, :] * scale - teacher[0, rows, :]).astype(BF16)
        fill_one_hot(codes, hot)

    def count(i, hot, grads, ranks):
        found = dot(grads[0 : ranks * half, :], hot[...], ((1,), (1,)))
        for r in range(ranks):
            for j in range(WIDTH // 128):
                at = pl.multiple_of((r * OWN + i) * half, half)
                hist[j, pl.ds(at, half), :] = found[
                    r * half : (r + 1) * half, j * 128 : (j + 1) * 128
                ]

    copies = [
        pltpu.make_async_copy(got_far.at[:, c * FEATS : (c + 1) * FEATS], got.at[c], sems.at[c])
        for c in range(CHUNKS)
    ]
    following = jnp.minimum(2 * s, OWN - 1)

    @pl.when(s == 0)
    def _():
        prepare(0, exps_even, teacher_even, even, hot_a, grads_a)
        for copy in copies:
            copy.start()
        for row in range(half):
            at = row * SLOTS + OWN
            spread[:, at : at + OWN, :] = jnp.zeros((CHUNKS, OWN, FEATS), F32)
        weight = jnp.max(jnp.abs(weights[...]), axis=0, keepdims=True)
        note = jnp.max(message[pl.ds(1, half, stride=2), :], axis=0, keepdims=True)
        lane = iota(weight.shape, 1)
        for pair in range(OWN // 2):
            at = OWN + 2 * pair
            held = jnp.where((lane == at) | (lane == at + 1), weight, 0.0)
            noted = jnp.where(lane // (2 * TARGETS) == at // 2, note, 0.0)
            second[pair] = jnp.maximum(jnp.max(held), jnp.max(noted))

    def step(ranks):
        count(2 * s - 2, hot_a, grads_a, ranks)
        prepare(2 * s - 1, exps_odd, teacher_odd, odd, hot_b, grads_b)
        count(2 * s - 1, hot_b, grads_b, ranks)
        prepare(following, exps_even, teacher_even, even, hot_a, grads_a)

    filled = second[jnp.maximum(s - 1, 0)] > 0.0

    @pl.when((s > 0) & filled)
    def _():
        step(CAP)

    @pl.when((s > 0) & jnp.logical_not(filled))
    def _():
        step(1)

    last = s == pl.num_programs(0) - 1

    def finish(slot, slots):
        rows = slice(slot * half, (slot + slots) * half)
        for c in range(CHUNKS):
            h_high, h_low = split_two(
                jnp.concatenate([hist[2 * c, rows, :], hist[2 * c + 1, rows, :]], axis=1)
            )
            both = jnp.concatenate([high[c], low[c]], axis=1)
            wide = dot(h_high, both)
            part = wide[:, 0:FEATS] + wide[:, FEATS:] + dot(h_low, high[c])
            for j in range(slots):
                spread[c, pl.ds(slot + j, half, stride=SLOTS), :] = part[j * half : (j + 1) * half]
            book = dot(got[c, rows, :], h_high, ((0,), (0,)))
            books[c] = book if slot == 0 else books[c] + book

    @pl.when(last)
    def _():
        for copy in copies:
            copy.wait()
        finish(0, OWN)

    for pair in range(OWN // 2):

        @pl.when(last & (second[pair] > 0.0))
        def _(pair=pair):
            finish(OWN + 2 * pair, 2)

    @pl.when(last)
    def _():
        devices = out.shape[0]
        keep = iota((ENTRIES, FEATS), 0) % 16 == iota((ENTRIES, FEATS), 1) // SUBDIM
        top = CHUNKS * SLOTS
        out[CHUNKS * CENTROIDS :, top:, :] = jnp.zeros(
            (devices - CHUNKS * CENTROIDS, BOOK_ROWS, 128), BF16
        )
        for c in range(CHUNKS):
            part = spread[c].reshape(devices, SLOTS, FEATS)
            out[:, c * SLOTS : (c + 1) * SLOTS, :] = part.astype(BF16)
            book = jnp.where(keep, books[c].T, 0.0)
            book = jnp.sum(book.reshape(CENTROIDS, 16, FEATS), axis=1)
            b_high = book.astype(BF16)
            b_rest = book - b_high.astype(F32)
            b_mid = b_rest.astype(BF16)
            b_low = b_rest - b_mid.astype(F32)
            row = iota((CENTROIDS, BOOK_ROWS, FEATS), 1)
            parts = jnp.where(row == 0, b_high.astype(F32)[:, None, :], 0.0)
            parts = jnp.where(row == 1, b_mid.astype(F32)[:, None, :], parts)
            parts = jnp.where(row == 2, b_low[:, None, :], parts)
            out[c * CENTROIDS : (c + 1) * CENTROIDS, top:, :] = parts.astype(BF16)


def book_body(returned, total):
    parts = returned[...].astype(F32)
    total[...] = jnp.broadcast_to(
        jnp.sum(jnp.sum(parts, axis=0), axis=0, keepdims=True), total.shape
    )


def norm_body(rows, normed):
    value = rows[0 : CHUNKS * CENTROIDS, :]
    mean = jnp.sum(value * value, keepdims=True) / (CENTROIDS * D)
    value = value * lax.rsqrt(mean + EPSILON)
    for c in range(CHUNKS):
        normed[:, c * FEATS : (c + 1) * FEATS] = value[c * CENTROIDS : (c + 1) * CENTROIDS]


def combine_body(chosen, returned, out):
    devices = returned.shape[0]
    for c in range(CHUNKS):
        rows = returned[:, c * SLOTS : (c + 1) * SLOTS, :].reshape(devices * SLOTS, FEATS)
        out[:, c * FEATS : (c + 1) * FEATS] = dot(chosen[...], rows).astype(BF16)


def whole(shape):
    return pl.BlockSpec(shape, lambda *_: (0,) * len(shape))


def exchange(value):
    return lax.all_to_all(value, BOTH, 0, 0, tiled=True)


def uncopied(value):
    return pltpu.with_memory_space_constraint(value, pltpu.VMEM)


def spread_codebook(codebook):
    book = codebook.reshape(CENTROIDS, CHUNKS, FEATS).transpose(1, 0, 2)
    own = jnp.arange(16)[:, None] == jnp.arange(FEATS)[None, :] // SUBDIM
    spread = jnp.where(own[None, None], book[:, :, None, :], 0.0)
    spread = spread.reshape(CHUNKS, ENTRIES, FEATS)
    high = lax.reduce_precision(spread, 8, 7)
    return high.astype(BF16), (spread - high).astype(BF16)


def shards(queries, probes, targets, passage_codes, codebook):
    devices = lax.axis_size("corpus") * lax.axis_size("query")
    count = queries.shape[0]
    slots = devices * SLOTS
    list_rows = devices * CAP
    probes_t = probes.T
    big = pltpu.CompilerParams(
        dimension_semantics=("arbitrary",), vmem_limit_bytes=58 * 1024 * 1024
    )
    square = jax.ShapeDtypeStruct((devices, 128), F32)

    sending = pl.pallas_call(
        dispatch_body,
        out_shape=jax.ShapeDtypeStruct((slots, D), BF16),
        grid=(2,),
        in_specs=[whole((PROBES, count)), whole((count, D))],
        out_specs=pl.BlockSpec((slots // 2, D), lambda b: (b, 0)),
        name="dispatch",
    )(probes_t, queries)
    got = uncopied(exchange(sending))
    arrived = pl.BlockSpec(memory_space=pl.ANY)
    arrived_here = pltpu.VMEM((CHUNKS, slots, FEATS), BF16)

    here = pl.BlockSpec(memory_space=pltpu.VMEM)
    scalars = pl.BlockSpec(memory_space=pltpu.SMEM)
    chosen, masks, notes, used = pl.pallas_call(
        home_body,
        out_shape=(
            jax.ShapeDtypeStruct((count, slots), BF16),
            jax.ShapeDtypeStruct((SLOTS, devices, count), BF16),
            square,
            jax.ShapeDtypeStruct((SLOTS,), jnp.int32),
        ),
        out_specs=(here, here, here, scalars),
        name="home",
    )(probes_t, probes, jnp.tile(targets, (1, 128 // TARGETS)))
    high, low = spread_codebook(codebook)
    offset = (lax.axis_index("query") * OWN).astype(jnp.int32).reshape(1)

    def code_of(index):
        return pl.BlockSpec(
            (1, SUBSPACES, PASSAGES), lambda s, off: (off[0] + index(s), 0, 0)
        )

    def in_order(index_of):
        return [
            index_of(lambda s: jnp.clip(2 * s - 1, 1, OWN - 1)),
            index_of(lambda s: jnp.minimum(2 * s, OWN - 1)),
        ]

    code_specs = in_order(code_of)
    table_spec = whole((CHUNKS, ENTRIES, FEATS))
    table = pltpu.VMEM((WIDTH // 128, slots, 128), F32)
    hot = pltpu.VMEM((WIDTH, PASSAGES), BF16)
    codes = (passage_codes,) * 2

    exps, message = pl.pallas_call(
        score_body,
        out_shape=(
            jax.ShapeDtypeStruct((OWN + 2, list_rows, PASSAGES), F32),
            jax.ShapeDtypeStruct((2 * devices, 128), F32),
        ),
        grid_spec=pltpu.PrefetchScalarGridSpec(
            num_scalar_prefetch=1,
            grid=(OWN // 2 + 2,),
            in_specs=[arrived, table_spec, table_spec, whole(square.shape)] + code_specs,
            out_specs=[
                pl.BlockSpec(
                    (2, list_rows, PASSAGES), lambda s, off: (jnp.maximum(s - 1, 0), 0, 0)
                ),
                whole((2 * devices, 128)),
            ],
            scratch_shapes=[table, hot, hot]
            + [pltpu.VMEM((list_rows, PASSAGES), F32)] * 2
            + [
                pltpu.VMEM(square.shape, F32),
                pltpu.VMEM((slots, D), BF16),
                pltpu.SMEM((OWN // 2,), F32),
                pltpu.SemaphoreType.DMA(()),
            ],
        ),
        compiler_params=big,
        name="score",
    )(offset, got, high, low, notes, *codes)

    message = uncopied(exchange(message))
    regrouped = pl.pallas_call(
        regroup_body,
        out_shape=jax.ShapeDtypeStruct((SLOTS, devices, D), BF16),
        grid=(devices // SLOTS,),
        in_specs=[pl.BlockSpec((SLOTS * SLOTS, D), lambda b: (b, 0))],
        out_specs=pl.BlockSpec((SLOTS, SLOTS, D), lambda b: (0, b, 0)),
        name="regroup",
    )(got).reshape(slots, D)
    weights = pl.pallas_call(
        weight_body,
        out_shape=square,
        in_specs=[scalars, here, here],
        scratch_shapes=[pltpu.VMEM((SLOTS, devices, count), F32)]
        + [pltpu.VMEM((devices, count), F32)] * 2,
        name="weigh",
    )(used, message, uncopied(masks))
    teacher = pl.pallas_call(
        teacher_body,
        out_shape=jax.ShapeDtypeStruct((OWN, list_rows, PASSAGES), F32),
        grid=(OWN,),
        in_specs=[whole((2 * devices, 128))],
        out_specs=pl.BlockSpec((1, list_rows, PASSAGES), lambda i: (i, 0, 0)),
        name="teacher",
    )(message)

    def exps_of(index):
        return pl.BlockSpec((1, list_rows, PASSAGES), lambda s, off: (index(s), 0, 0))

    result = pl.pallas_call(
        grad_body,
        out_shape=jax.ShapeDtypeStruct((devices, CHUNKS * SLOTS + BOOK_ROWS, FEATS), BF16),
        grid_spec=pltpu.PrefetchScalarGridSpec(
            num_scalar_prefetch=1,
            grid=(OWN // 2 + 1,),
            in_specs=[
                whole(square.shape),
                whole((2 * devices, 128)),
                arrived,
                table_spec,
                table_spec,
            ]
            + in_order(lambda index: exps_of(lambda s: index(s) + 1))
            + in_order(exps_of)
            + code_specs,
            out_specs=whole((devices, CHUNKS * SLOTS + BOOK_ROWS, FEATS)),
            scratch_shapes=[table, hot, hot]
            + [pltpu.VMEM((list_rows, PASSAGES), BF16)] * 2
            + [
                arrived_here,
                pltpu.SMEM((OWN // 2,), F32),
                pltpu.VMEM((CHUNKS, slots, FEATS), F32),
                pltpu.VMEM((CHUNKS, FEATS, ENTRIES), F32),
                pltpu.SemaphoreType.DMA((CHUNKS,)),
            ],
        ),
        compiler_params=big,
        name="grad",
    )(
        offset, uncopied(exchange(weights)), message, regrouped, high, low,
        exps, exps, teacher, teacher, *codes,
    )

    returned = exchange(result)
    book_spec = pl.BlockSpec(
        (devices, BOOK_ROWS, FEATS), lambda b: (0, CHUNKS * SLOTS // BOOK_ROWS, 0)
    )
    book_sum = pl.pallas_call(
        book_body,
        out_shape=square,
        grid=(1,),
        in_specs=[book_spec],
        out_specs=whole(square.shape),
        name="book_sum",
    )(returned)
    normed = pl.pallas_call(
        norm_body, out_shape=jax.ShapeDtypeStruct((CENTROIDS, D), F32), name="book_norm"
    )(uncopied(exchange(book_sum)))
    grad_queries = pl.pallas_call(
        combine_body,
        out_shape=jax.ShapeDtypeStruct((count, D), BF16),
        grid=(1,),
        in_specs=[
            whole((count, slots)),
            pl.BlockSpec((devices, CHUNKS * SLOTS, FEATS), lambda b: (0, 0, 0)),
        ],
        out_specs=whole((count, D)),
        name="combine",
    )(chosen, returned)
    return grad_queries, normed


def solution(mesh):
    placed = (
        P(BOTH, None),
        P(BOTH, None),
        P(BOTH, None),
        P("corpus", None, None),
        P(),
    )

    return jax.shard_map(
        shards,
        mesh=mesh,
        in_specs=placed,
        out_specs=(P(BOTH, None), P()),
        check_vma=False,
    )
```
